256 devices in a mesh: batch: 2 (over z_lo), seq: 128 (over z_hi, y, x, core).
Axes of the slice: x: 4, y: 4, z: 8 (z_hi: 4, z_lo: 2; z = z_hi * 2 + z_lo), core: 2. Of those that a mesh axis runs over, the one named last changes fastest.
Arguments:
- signal: bfloat16 [2, 262144, 384], P('batch', 'seq'), may hold values from -6 to 6
- conv_weight: float32 [4, 384], replicated, may hold values from -2.5 to 2.5
- first_factor: bfloat16 [512, 512, 512], P('seq'), may hold values from -0.25 to 0.25
- second_factor: bfloat16 [512, 512, 512], P('seq'), may hold values from -0.25 to 0.25
- grad_output: bfloat16 [2, 262144, 384], P('batch', 'seq'), may hold values from -3 to 3
Outputs:
- grad_signal: bfloat16 [2, 262144, 384], P('batch', 'seq')
- grad_first: bfloat16 [512, 512, 512], P('seq', 'batch')
- grad_second: bfloat16 [512, 512, 512], P('seq', 'batch')
The draws below stay inside these ranges and needn't reach their ends.
All inputs are finite; a program needn't handle non-finite values.
Results may differ from the reference program's by a relative error of at most 0.0065.
Values may be sent and summed in bfloat16 or wider, within the bound.
A program may use at most 128 MiB of HBM per device.

```python
import jax
import jax.numpy as jnp
from jax import lax

D = 384
NB = 512
BS = 512
KW = 4
SEQ_DEV = 1
L = 262144
NSEQ = 2
N_BATCH = 2


def block_levels(own_key, dims, shards, least, top_value):
    factor_of, own = 1.0, jax.random.fold_in(own_key, 6)
    for dim, parts in shards:
        steps = jnp.exp(jax.random.uniform(jax.random.fold_in(own, dim), (parts,), jnp.float32, least / len(shards), top_value / len(shards)))
        factor_of = factor_of * jnp.repeat(steps, dims[dim] // parts).reshape([-1 if axis == dim else 1 for axis in range(len(dims))])
    return factor_of


def centred(stream_key, extent, width, bound, shards=(), held_as=jnp.bfloat16):
    gain = block_levels(stream_key, extent, shards, -0.22, 0.18) if shards else 1.0
    entries = jax.random.normal(stream_key, extent, jnp.float32) * width * gain
    return jnp.minimum(jnp.maximum(entries, -bound), bound).astype(held_as)


def setup_inputs(seed: int = 0) -> dict:
    arg_keys = jax.random.split(jax.random.key(seed), 6)
    return {
        "signal": centred(arg_keys[0], (NSEQ, L, D), 1.0, 6.0, ((0, 2), (1, 128))),
        "conv_weight": centred(arg_keys[1], (KW, D), 0.5, 2.5, (), jnp.float32),
        "first_factor": centred(arg_keys[2], (NB, BS, BS), BS ** -0.5, 0.25, ((0, 128),)),
        "second_factor": centred(arg_keys[3], (BS, NB, NB), NB ** -0.5, 0.25, ((0, 128),)),
        "grad_output": centred(arg_keys[4], (NSEQ, L, D), 0.5, 3.0, ((0, 2), (1, 128))),
    }


def reference(signal, conv_weight, first_factor, second_factor, grad_output):
    seq_count = signal.shape[0]
    signal_f = signal.astype(jnp.float32)
    padded_in = jnp.pad(signal_f, ((0, 0), (KW - 1, 0), (0, 0)))
    conv_out = sum(conv_weight[r][None, None, :] * padded_in[:, KW - 1 - r:KW - 1 - r + L, :] for r in range(KW))
    gate_val = jax.nn.sigmoid(conv_out)
    hidden = (conv_out * gate_val).astype(jnp.bfloat16)
    hidden_blocks = hidden.reshape(seq_count, NB, BS, D)
    first_f = first_factor.astype(jnp.float32)
    second_f = second_factor.astype(jnp.float32)
    mixed = jnp.einsum('ikj,sijd->sikd', first_f, hidden_blocks.astype(jnp.float32)).astype(jnp.bfloat16)
    upstream = grad_output.reshape(seq_count, BS, NB, D)
    grad_mixed = jnp.einsum('kmi,skmd->sikd', second_f, upstream.astype(jnp.float32)).astype(jnp.bfloat16)
    grad_hidden = jnp.einsum('ikj,sikd->sijd', first_f, grad_mixed.astype(jnp.float32)).reshape(seq_count, L, D)
    grad_conv = (grad_hidden * gate_val * (1.0 + conv_out * (1.0 - gate_val))).astype(jnp.bfloat16)
    padded_back = jnp.pad(grad_conv.astype(jnp.float32), ((0, 0), (0, KW - 1), (0, 0)))
    grad_signal = sum(conv_weight[r][None, None, :] * padded_back[:, r:r + L, :] for r in range(KW)).astype(jnp.bfloat16)
    total_first = jnp.zeros((NB, BS, BS), jnp.float32)
    total_second = jnp.zeros((BS, NB, NB), jnp.float32)
    for group in range(N_BATCH):
        low = group * SEQ_DEV
        part_mixed = grad_mixed[low:low + SEQ_DEV].astype(jnp.float32)
        part_hidden = hidden_blocks[low:low + SEQ_DEV].astype(jnp.float32)
        part_up = upstream[low:low + SEQ_DEV].astype(jnp.float32)
        part_fwd = mixed[low:low + SEQ_DEV].astype(jnp.float32)
        part_first = jnp.einsum('sikd,sijd->ikj', part_mixed, part_hidden).astype(jnp.bfloat16)
        part_second = jnp.einsum('skmd,sikd->kmi', part_up, part_fwd).astype(jnp.bfloat16)
        total_first = total_first + lax.optimization_barrier(part_first).astype(jnp.float32)
        total_second = total_second + lax.optimization_barrier(part_second).astype(jnp.float32)
    return grad_signal, total_first.astype(jnp.bfloat16), total_second.astype(jnp.bfloat16)
```

```python
import jax
import jax.numpy as jnp
from jax import lax
from jax.sharding import PartitionSpec as P


def passed_along(value, axis, steps):
    count = lax.axis_size(axis)
    initial, last = (max(0, -steps), min(count, count - steps))
    return lax.ppermute(value, axis, [(source, source + steps) for source in range(initial, last)])


def body(signal, conv_weight, first_factor, second_factor, grad_output):
    seq_count, tok_rows, channels = signal.shape
    blocks = first_factor.shape[0]
    block_order = first_factor.shape[1]
    col_blocks = second_factor.shape[0]
    block_count = second_factor.shape[1]
    tap_count = conv_weight.shape[0]
    peers = lax.axis_size("seq")
    previous = passed_along(signal[:, tok_rows - (tap_count - 1) :, :], "seq", 1)
    padded_in = jnp.concatenate([previous, signal], axis=1).astype(jnp.float32)
    conv_out = sum(
        (
            conv_weight[r][None, None, :]
            * padded_in[:, tap_count - 1 - r : tap_count - 1 - r + tok_rows, :]
            for r in range(tap_count)
        )
    )
    gate_val = jax.nn.sigmoid(conv_out)
    hidden = (conv_out * gate_val).astype(jnp.bfloat16)
    hidden_blocks = hidden.reshape(seq_count, blocks, block_order, channels)
    first_split = first_factor.reshape(blocks, peers, col_blocks, block_order)
    mixed_chunks = jnp.einsum(
        "ipqj,sijd->psiqd", first_split, hidden_blocks, preferred_element_type=jnp.float32
    ).astype(jnp.bfloat16)
    upstream = grad_output.reshape(seq_count, col_blocks, block_count, channels)
    second_split = second_factor.reshape(col_blocks, block_count, peers, blocks)
    grad_chunks = jnp.einsum(
        "kmpi,skmd->psikd", second_split, upstream, preferred_element_type=jnp.float32
    ).astype(jnp.bfloat16)
    sent = jnp.stack([mixed_chunks, grad_chunks], axis=1)
    got = lax.all_to_all(sent, "seq", split_axis=0, concat_axis=0, tiled=True)
    columns = got[:, 0]
    grad_rows = got[:, 1]
    halves = lax.axis_size("batch")
    me = lax.axis_index("batch")
    other = halves - 1 - me
    rows_half = block_count // halves
    peers_half = peers // halves

    def second_part(half):
        up = lax.dynamic_slice_in_dim(upstream, half * rows_half, rows_half, 2)
        return jnp.einsum(
            "skmd,psikd->kmpi", up, columns, preferred_element_type=jnp.float32
        ).reshape(col_blocks, rows_half, peers * blocks).astype(jnp.bfloat16)

    def first_part(half):
        gr = lax.dynamic_slice_in_dim(grad_rows, half * peers_half, peers_half, 0)
        return jnp.einsum(
            "psiqd,sijd->ipqj", gr, hidden_blocks, preferred_element_type=jnp.float32
        ).reshape(blocks, peers_half * col_blocks, block_order).astype(jnp.bfloat16)

    swap = [(0, 1), (1, 0)]
    sent_second = lax.ppermute(second_part(other), "batch", swap)
    sent_first = lax.ppermute(first_part(other), "batch", swap)
    grad_hidden = jnp.einsum(
        "ipqj,psiqd->sijd", first_split, grad_rows, preferred_element_type=jnp.float32
    ).reshape(seq_count, tok_rows, channels)
    part_second = (
        second_part(me).astype(jnp.float32) + sent_second.astype(jnp.float32)
    ).astype(jnp.bfloat16)
    part_first = (
        first_part(me).astype(jnp.float32) + sent_first.astype(jnp.float32)
    ).astype(jnp.bfloat16)
    grad_conv = (grad_hidden * gate_val * (1.0 + conv_out * (1.0 - gate_val))).astype(jnp.bfloat16)
    following = passed_along(grad_conv[:, : tap_count - 1, :], "seq", -1)
    extended = jnp.concatenate([grad_conv, following], axis=1).astype(jnp.float32)
    grad_signal = sum(
        (conv_weight[r][None, None, :] * extended[:, r : r + tok_rows, :] for r in range(tap_count))
    ).astype(jnp.bfloat16)
    return (grad_signal, part_first, part_second)


def solution(mesh):
    placed = (
        P("batch", "seq", None),
        P(),
        P("seq", None, None),
        P("seq", None, None),
        P("batch", "seq", None),
    )
    return jax.shard_map(
        body,
        mesh=mesh,
        in_specs=placed,
        out_specs=(P("batch", "seq", None), P("seq", "batch", None), P("seq", "batch", None)),
        check_vma=False,
    )
```

```python
import jax
import jax.numpy as jnp
from jax import lax
from jax.sharding import PartitionSpec as P


def passed_along(value, axis, steps):
    count = lax.axis_size(axis)
    initial, last = (max(0, -steps), min(count, count - steps))
    return lax.ppermute(value, axis, [(source, source + steps) for source in range(initial, last)])


def body(signal, conv_weight, first_factor, second_factor, grad_output):
    seq_count, tok_rows, channels = signal.shape
    blocks = first_factor.shape[0]
    block_order = first_factor.shape[1]
    col_blocks = second_factor.shape[0]
    block_count = second_factor.shape[1]
    tap_count = conv_weight.shape[0]
    peers = lax.axis_size("seq")
    previous = passed_along(signal[:, tok_rows - (tap_count - 1) :, :], "seq", 1)
    padded_in = jnp.concatenate([previous, signal], axis=1).astype(jnp.float32)
    conv_out = sum(
        (
            conv_weight[r][None, None, :]
            * padded_in[:, tap_count - 1 - r : tap_count - 1 - r + tok_rows, :]
            for r in range(tap_count)
        )
    )
    gate_val = jax.nn.sigmoid(conv_out)
    hidden = (conv_out * gate_val).astype(jnp.bfloat16)
    hidden_blocks = hidden.reshape(seq_count, blocks, block_order, channels)
    first_split = first_factor.reshape(blocks, peers, col_blocks, block_order)
    mixed_chunks = jnp.einsum(
        "ipqj,sijd->psiqd", first_split, hidden_blocks, preferred_element_type=jnp.float32
    ).astype(jnp.bfloat16)
    upstream = grad_output.reshape(seq_count, col_blocks, block_count, channels)
    second_split = second_factor.reshape(col_blocks, block_count, peers, blocks)
    grad_chunks = jnp.einsum(
        "kmpi,skmd->psikd", second_split, upstream, preferred_element_type=jnp.float32
    ).astype(jnp.bfloat16)
    grad_rows = lax.all_to_all(grad_chunks, "seq", split_axis=0, concat_axis=0, tiled=True)
    columns = lax.all_to_all(mixed_chunks, "seq", split_axis=0, concat_axis=0, tiled=True)
    halves = lax.axis_size("batch")
    me = lax.axis_index("batch")
    other = halves - 1 - me
    rows_half = block_count // halves
    peers_half = peers // halves

    def second_part(half):
        up = lax.dynamic_slice_in_dim(upstream, half * rows_half, rows_half, 2)
        return jnp.einsum(
            "skmd,psikd->kmpi", up, columns, preferred_element_type=jnp.float32
        ).reshape(col_blocks, rows_half, peers * blocks).astype(jnp.bfloat16)

    def first_part(half):
        gr = lax.dynamic_slice_in_dim(grad_rows, half * peers_half, peers_half, 0)
        return jnp.einsum(
            "psiqd,sijd->ipqj", gr, hidden_blocks, preferred_element_type=jnp.float32
        ).reshape(blocks, peers_half * col_blocks, block_order).astype(jnp.bfloat16)

    swap = [(0, 1), (1, 0)]
    sent_second = lax.ppermute(second_part(other), "batch", swap)
    sent_first = lax.ppermute(first_part(other), "batch", swap)
    grad_hidden = jnp.einsum(
        "ipqj,psiqd->sijd", first_split, grad_rows, preferred_element_type=jnp.float32
    ).reshape(seq_count, tok_rows, channels)
    part_second = (
        second_part(me).astype(jnp.float32) + sent_second.astype(jnp.float32)
    ).astype(jnp.bfloat16)
    part_first = (
        first_part(me).astype(jnp.float32) + sent_first.astype(jnp.float32)
    ).astype(jnp.bfloat16)
    grad_conv = (grad_hidden * gate_val * (1.0 + conv_out * (1.0 - gate_val))).astype(jnp.bfloat16)
    following = passed_along(grad_conv[:, : tap_count - 1, :], "seq", -1)
    extended = jnp.concatenate([grad_conv, following], axis=1).astype(jnp.float32)
    grad_signal = sum(
        (conv_weight[r][None, None, :] * extended[:, r : r + tok_rows, :] for r in range(tap_count))
    ).astype(jnp.bfloat16)
    return (grad_signal, part_first, part_second)


def solution(mesh):
    placed = (
        P("batch", "seq", None),
        P(),
        P("seq", None, None),
        P("seq", None, None),
        P("batch", "seq", None),
    )
    return jax.shard_map(
        body,
        mesh=mesh,
        in_specs=placed,
        out_specs=(P("batch", "seq", None), P("seq", "batch", None), P("seq", "batch", None)),
        check_vma=False,
    )
```

```python
import jax
import jax.numpy as jnp
from jax import lax
from jax.sharding import PartitionSpec as P
from jax.experimental import pallas as pl
from jax.experimental.pallas import tpu as pltpu
import functools

MESH = pl.DeviceIdType.MESH


def _a2a_kernel(n, x_ref, o_ref, send_sem, recv_sem, local_sem):
    me = lax.axis_index("seq")
    barrier = pltpu.get_barrier_semaphore()

    def greet(j, carry):
        peer = lax.rem(me + j, n)
        pl.semaphore_signal(barrier, inc=1, device_id={"seq": peer}, device_id_type=MESH)
        return carry

    lax.fori_loop(1, n, greet, 0)
    pl.semaphore_wait(barrier, n - 1)
    local = pltpu.make_async_copy(x_ref.at[me], o_ref.at[me], local_sem)
    local.start()

    def outgoing(j):
        peer = lax.rem(me + j, n)
        return pltpu.make_async_remote_copy(
            src_ref=x_ref.at[peer],
            dst_ref=o_ref.at[me],
            send_sem=send_sem.at[peer],
            recv_sem=recv_sem.at[me],
            device_id={"seq": peer},
            device_id_type=MESH,
        )

    def incoming(j):
        source = lax.rem(me + n - j, n)
        return pltpu.make_async_remote_copy(
            src_ref=x_ref.at[me],
            dst_ref=o_ref.at[source],
            send_sem=send_sem.at[source],
            recv_sem=recv_sem.at[source],
            device_id={"seq": source},
            device_id_type=MESH,
        )

    def send(j, carry):
        outgoing(j).start()
        return carry

    lax.fori_loop(1, n, send, 0)

    def drain(j, carry):
        outgoing(j).wait_send()
        incoming(j).wait_recv()
        return carry

    lax.fori_loop(1, n, drain, 0)
    local.wait()


def all_to_all(x, n, cid):
    return pl.pallas_call(
        functools.partial(_a2a_kernel, n),
        out_shape=jax.ShapeDtypeStruct(x.shape, x.dtype),
        in_specs=[pl.BlockSpec(memory_space=pl.ANY)],
        out_specs=pl.BlockSpec(memory_space=pl.ANY),
        scratch_shapes=[
            pltpu.SemaphoreType.DMA((n,)),
            pltpu.SemaphoreType.DMA((n,)),
            pltpu.SemaphoreType.DMA(()),
        ],
        compiler_params=pltpu.CompilerParams(collective_id=cid, has_side_effects=True),
    )(x)


def passed_along(value, axis, steps):
    count = lax.axis_size(axis)
    initial, last = (max(0, -steps), min(count, count - steps))
    return lax.ppermute(value, axis, [(source, source + steps) for source in range(initial, last)])


def body(signal, conv_weight, first_factor, second_factor, grad_output):
    seq_count, tok_rows, channels = signal.shape
    blocks = first_factor.shape[0]
    block_order = first_factor.shape[1]
    col_blocks = second_factor.shape[0]
    block_count = second_factor.shape[1]
    tap_count = conv_weight.shape[0]
    peers = lax.axis_size("seq")
    previous = passed_along(signal[:, tok_rows - (tap_count - 1) :, :], "seq", 1)
    padded_in = jnp.concatenate([previous, signal], axis=1).astype(jnp.float32)
    conv_out = sum(
        (
            conv_weight[r][None, None, :]
            * padded_in[:, tap_count - 1 - r : tap_count - 1 - r + tok_rows, :]
            for r in range(tap_count)
        )
    )
    gate_val = jax.nn.sigmoid(conv_out)
    hidden = (conv_out * gate_val).astype(jnp.bfloat16)
    hidden_blocks = hidden.reshape(seq_count, blocks, block_order, channels)
    first_split = first_factor.reshape(blocks, peers, col_blocks, block_order)
    mixed_chunks = jnp.einsum(
        "ipqj,sijd->psiqd", first_split, hidden_blocks, preferred_element_type=jnp.float32
    ).astype(jnp.bfloat16)
    upstream = grad_output.reshape(seq_count, col_blocks, block_count, channels)
    second_split = second_factor.reshape(col_blocks, block_count, peers, blocks)
    grad_chunks = jnp.einsum(
        "kmpi,skmd->psikd", second_split, upstream, preferred_element_type=jnp.float32
    ).astype(jnp.bfloat16)
    grad_rows = all_to_all(grad_chunks, peers, 0)
    columns = all_to_all(mixed_chunks, peers, 1)
    halves = lax.axis_size("batch")
    me = lax.axis_index("batch")
    other = halves - 1 - me
    rows_half = block_count // halves
    peers_half = peers // halves

    def second_part(half):
        up = lax.dynamic_slice_in_dim(upstream, half * rows_half, rows_half, 2)
        return jnp.einsum(
            "skmd,psikd->kmpi", up, columns, preferred_element_type=jnp.float32
        ).reshape(col_blocks, rows_half, peers * blocks).astype(jnp.bfloat16)

    def first_part(half):
        gr = lax.dynamic_slice_in_dim(grad_rows, half * peers_half, peers_half, 0)
        return jnp.einsum(
            "psiqd,sijd->ipqj", gr, hidden_blocks, preferred_element_type=jnp.float32
        ).reshape(blocks, peers_half * col_blocks, block_order).astype(jnp.bfloat16)

    swap = [(0, 1), (1, 0)]
    sent_second = lax.ppermute(second_part(other), "batch", swap)
    sent_first = lax.ppermute(first_part(other), "batch", swap)
    grad_hidden = jnp.einsum(
        "ipqj,psiqd->sijd", first_split, grad_rows, preferred_element_type=jnp.float32
    ).reshape(seq_count, tok_rows, channels)
    part_second = (
        second_part(me).astype(jnp.float32) + sent_second.astype(jnp.float32)
    ).astype(jnp.bfloat16)
    part_first = (
        first_part(me).astype(jnp.float32) + sent_first.astype(jnp.float32)
    ).astype(jnp.bfloat16)
    grad_conv = (grad_hidden * gate_val * (1.0 + conv_out * (1.0 - gate_val))).astype(jnp.bfloat16)
    following = passed_along(grad_conv[:, : tap_count - 1, :], "seq", -1)
    extended = jnp.concatenate([grad_conv, following], axis=1).astype(jnp.float32)
    grad_signal = sum(
        (conv_weight[r][None, None, :] * extended[:, r : r + tok_rows, :] for r in range(tap_count))
    ).astype(jnp.bfloat16)
    return (grad_signal, part_first, part_second)


def solution(mesh):
    placed = (
        P("batch", "seq", None),
        P(),
        P("seq", None, None),
        P("seq", None, None),
        P("batch", "seq", None),
    )
    return jax.shard_map(
        body,
        mesh=mesh,
        in_specs=placed,
        out_specs=(P("batch", "seq", None), P("seq", "batch", None), P("seq", "batch", None)),
        check_vma=False,
    )
```

```python
import jax
import jax.numpy as jnp
from jax import lax
from jax.sharding import PartitionSpec as P
from jax.experimental import pallas as pl
from jax.experimental.pallas import tpu as pltpu
import functools

MESH = pl.DeviceIdType.MESH


def _a2a_kernel(n, x_refs, o_refs, send_sem, recv_sem, local_sem):
    me = lax.axis_index("seq")
    barrier = pltpu.get_barrier_semaphore()

    def greet(j, carry):
        peer = lax.rem(me + j, n)
        pl.semaphore_signal(barrier, inc=1, device_id={"seq": peer}, device_id_type=MESH)
        return carry

    lax.fori_loop(1, n, greet, 0)
    pl.semaphore_wait(barrier, n - 1)
    count = len(x_refs)
    locals_ = [
        pltpu.make_async_copy(x_refs[c].at[me], o_refs[c].at[me], local_sem.at[c])
        for c in range(count)
    ]
    for copy in locals_:
        copy.start()

    def outgoing(c, j):
        peer = lax.rem(me + j, n)
        return pltpu.make_async_remote_copy(
            src_ref=x_refs[c].at[peer],
            dst_ref=o_refs[c].at[me],
            send_sem=send_sem.at[c, peer],
            recv_sem=recv_sem.at[c, me],
            device_id={"seq": peer},
            device_id_type=MESH,
        )

    def incoming(c, j):
        source = lax.rem(me + n - j, n)
        return pltpu.make_async_remote_copy(
            src_ref=x_refs[c].at[me],
            dst_ref=o_refs[c].at[source],
            send_sem=send_sem.at[c, source],
            recv_sem=recv_sem.at[c, source],
            device_id={"seq": source},
            device_id_type=MESH,
        )

    def send(j, carry):
        for c in range(count):
            outgoing(c, j).start()
        return carry

    lax.fori_loop(1, n, send, 0)

    def drain(j, carry):
        for c in range(count):
            outgoing(c, j).wait_send()
            incoming(c, j).wait_recv()
        return carry

    lax.fori_loop(1, n, drain, 0)
    for copy in locals_:
        copy.wait()


def all_to_all(xs, n, cid):
    count = len(xs)

    def kernel(*refs):
        _a2a_kernel(n, refs[:count], refs[count : 2 * count], *refs[2 * count :])

    return pl.pallas_call(
        kernel,
        out_shape=[jax.ShapeDtypeStruct(x.shape, x.dtype) for x in xs],
        in_specs=[pl.BlockSpec(memory_space=pl.ANY)] * count,
        out_specs=[pl.BlockSpec(memory_space=pl.ANY)] * count,
        scratch_shapes=[
            pltpu.SemaphoreType.DMA((count, n)),
            pltpu.SemaphoreType.DMA((count, n)),
            pltpu.SemaphoreType.DMA((count,)),
        ],
        compiler_params=pltpu.CompilerParams(collective_id=cid, has_side_effects=True),
    )(*xs)


def passed_along(value, axis, steps):
    count = lax.axis_size(axis)
    initial, last = (max(0, -steps), min(count, count - steps))
    return lax.ppermute(value, axis, [(source, source + steps) for source in range(initial, last)])


def body(signal, conv_weight, first_factor, second_factor, grad_output):
    seq_count, tok_rows, channels = signal.shape
    blocks = first_factor.shape[0]
    block_order = first_factor.shape[1]
    col_blocks = second_factor.shape[0]
    block_count = second_factor.shape[1]
    tap_count = conv_weight.shape[0]
    peers = lax.axis_size("seq")
    previous = passed_along(signal[:, tok_rows - (tap_count - 1) :, :], "seq", 1)
    padded_in = jnp.concatenate([previous, signal], axis=1).astype(jnp.float32)
    conv_out = sum(
        (
            conv_weight[r][None, None, :]
            * padded_in[:, tap_count - 1 - r : tap_count - 1 - r + tok_rows, :]
            for r in range(tap_count)
        )
    )
    gate_val = jax.nn.sigmoid(conv_out)
    hidden = (conv_out * gate_val).astype(jnp.bfloat16)
    hidden_blocks = hidden.reshape(seq_count, blocks, block_order, channels)
    first_split = first_factor.reshape(blocks, peers, col_blocks, block_order)
    mixed_chunks = jnp.einsum(
        "ipqj,sijd->psiqd", first_split, hidden_blocks, preferred_element_type=jnp.float32
    ).astype(jnp.bfloat16)
    upstream = grad_output.reshape(seq_count, col_blocks, block_count, channels)
    second_split = second_factor.reshape(col_blocks, block_count, peers, blocks)
    grad_chunks = jnp.einsum(
        "kmpi,skmd->psikd", second_split, upstream, preferred_element_type=jnp.float32
    ).astype(jnp.bfloat16)
    grad_rows, columns = all_to_all([grad_chunks, mixed_chunks], peers, 0)
    halves = lax.axis_size("batch")
    me = lax.axis_index("batch")
    other = halves - 1 - me
    rows_half = block_count // halves
    peers_half = peers // halves

    def second_part(half):
        up = lax.dynamic_slice_in_dim(upstream, half * rows_half, rows_half, 2)
        return jnp.einsum(
            "skmd,psikd->kmpi", up, columns, preferred_element_type=jnp.float32
        ).reshape(col_blocks, rows_half, peers * blocks).astype(jnp.bfloat16)

    def first_part(half):
        gr = lax.dynamic_slice_in_dim(grad_rows, half * peers_half, peers_half, 0)
        return jnp.einsum(
            "psiqd,sijd->ipqj", gr, hidden_blocks, preferred_element_type=jnp.float32
        ).reshape(blocks, peers_half * col_blocks, block_order).astype(jnp.bfloat16)

    swap = [(0, 1), (1, 0)]
    sent_second = lax.ppermute(second_part(other), "batch", swap)
    sent_first = lax.ppermute(first_part(other), "batch", swap)
    grad_hidden = jnp.einsum(
        "ipqj,psiqd->sijd", first_split, grad_rows, preferred_element_type=jnp.float32
    ).reshape(seq_count, tok_rows, channels)
    part_second = (
        second_part(me).astype(jnp.float32) + sent_second.astype(jnp.float32)
    ).astype(jnp.bfloat16)
    part_first = (
        first_part(me).astype(jnp.float32) + sent_first.astype(jnp.float32)
    ).astype(jnp.bfloat16)
    grad_conv = (grad_hidden * gate_val * (1.0 + conv_out * (1.0 - gate_val))).astype(jnp.bfloat16)
    following = passed_along(grad_conv[:, : tap_count - 1, :], "seq", -1)
    extended = jnp.concatenate([grad_conv, following], axis=1).astype(jnp.float32)
    grad_signal = sum(
        (conv_weight[r][None, None, :] * extended[:, r : r + tok_rows, :] for r in range(tap_count))
    ).astype(jnp.bfloat16)
    return (grad_signal, part_first, part_second)


def solution(mesh):
    placed = (
        P("batch", "seq", None),
        P(),
        P("seq", None, None),
        P("seq", None, None),
        P("batch", "seq", None),
    )
    return jax.shard_map(
        body,
        mesh=mesh,
        in_specs=placed,
        out_specs=(P("batch", "seq", None), P("seq", "batch", None), P("seq", "batch", None)),
        check_vma=False,
    )
```

```python
import jax
import jax.numpy as jnp
from jax import lax
from jax.sharding import PartitionSpec as P
from jax.experimental import pallas as pl
from jax.experimental.pallas import tpu as pltpu


def _grad_payload_kernel(s_ref, g_ref, o_ref):
    width = g_ref.shape[-1]
    for k in range(s_ref.shape[0]):
        product = lax.dot_general(
            s_ref[k], g_ref[k], (((0,), (0,)), ((), ())), preferred_element_type=jnp.float32
        )
        o_ref[:, k * width : (k + 1) * width] = product.astype(o_ref.dtype)


def grad_payload(second_factor, upstream):
    col_blocks, rows, order = second_factor.shape
    width = upstream.shape[-1]
    flops = 2 * col_blocks * rows * order * width
    return pl.pallas_call(
        _grad_payload_kernel,
        out_shape=jax.ShapeDtypeStruct((order, col_blocks * width), jnp.bfloat16),
        in_specs=[pl.BlockSpec(memory_space=pltpu.VMEM)] * 2,
        out_specs=pl.BlockSpec(memory_space=pltpu.VMEM),
        cost_estimate=pl.CostEstimate(
            flops=flops, transcendentals=0, bytes_accessed=2 * (second_factor.size + 2 * upstream.size)
        ),
    )(second_factor, upstream.reshape(col_blocks, rows, width))


def passed_along(value, axis, steps):
    count = lax.axis_size(axis)
    initial, last = (max(0, -steps), min(count, count - steps))
    return lax.ppermute(value, axis, [(source, source + steps) for source in range(initial, last)])


def body(signal, conv_weight, first_factor, second_factor, grad_output):
    seq_count, tok_rows, channels = signal.shape
    blocks = first_factor.shape[0]
    block_order = first_factor.shape[1]
    col_blocks = second_factor.shape[0]
    block_count = second_factor.shape[1]
    tap_count = conv_weight.shape[0]
    peers = lax.axis_size("seq")
    previous = passed_along(signal[:, tok_rows - (tap_count - 1) :, :], "seq", 1)
    padded_in = jnp.concatenate([previous, signal], axis=1).astype(jnp.float32)
    conv_out = sum(
        (
            conv_weight[r][None, None, :]
            * padded_in[:, tap_count - 1 - r : tap_count - 1 - r + tok_rows, :]
            for r in range(tap_count)
        )
    )
    gate_val = jax.nn.sigmoid(conv_out)
    hidden = (conv_out * gate_val).astype(jnp.bfloat16)
    hidden_blocks = hidden.reshape(seq_count, blocks, block_order, channels)
    first_split = first_factor.reshape(blocks, peers, col_blocks, block_order)
    mixed_chunks = jnp.einsum(
        "ipqj,sijd->psiqd", first_split, hidden_blocks, preferred_element_type=jnp.float32
    ).astype(jnp.bfloat16)
    upstream = grad_output.reshape(seq_count, col_blocks, block_count, channels)
    grad_chunks = grad_payload(second_factor, upstream).reshape(
        peers, seq_count, blocks, col_blocks, channels
    )
    grad_rows = lax.all_to_all(grad_chunks, "seq", split_axis=0, concat_axis=0, tiled=True)
    columns = lax.all_to_all(mixed_chunks, "seq", split_axis=0, concat_axis=0, tiled=True)
    halves = lax.axis_size("batch")
    me = lax.axis_index("batch")
    other = halves - 1 - me
    rows_half = block_count // halves
    peers_half = peers // halves

    def second_part(half):
        up = lax.dynamic_slice_in_dim(upstream, half * rows_half, rows_half, 2)
        return jnp.einsum(
            "skmd,psikd->kmpi", up, columns, preferred_element_type=jnp.float32
        ).reshape(col_blocks, rows_half, peers * blocks).astype(jnp.bfloat16)

    def first_part(half):
        gr = lax.dynamic_slice_in_dim(grad_rows, half * peers_half, peers_half, 0)
        return jnp.einsum(
            "psiqd,sijd->ipqj", gr, hidden_blocks, preferred_element_type=jnp.float32
        ).reshape(blocks, peers_half * col_blocks, block_order).astype(jnp.bfloat16)

    swap = [(0, 1), (1, 0)]
    sent_second = lax.ppermute(second_part(other), "batch", swap)
    sent_first = lax.ppermute(first_part(other), "batch", swap)
    grad_hidden = jnp.einsum(
        "ipqj,psiqd->sijd", first_split, grad_rows, preferred_element_type=jnp.float32
    ).reshape(seq_count, tok_rows, channels)
    part_second = (
        second_part(me).astype(jnp.float32) + sent_second.astype(jnp.float32)
    ).astype(jnp.bfloat16)
    part_first = (
        first_part(me).astype(jnp.float32) + sent_first.astype(jnp.float32)
    ).astype(jnp.bfloat16)
    grad_conv = (grad_hidden * gate_val * (1.0 + conv_out * (1.0 - gate_val))).astype(jnp.bfloat16)
    following = passed_along(grad_conv[:, : tap_count - 1, :], "seq", -1)
    extended = jnp.concatenate([grad_conv, following], axis=1).astype(jnp.float32)
    grad_signal = sum(
        (conv_weight[r][None, None, :] * extended[:, r : r + tok_rows, :] for r in range(tap_count))
    ).astype(jnp.bfloat16)
    return (grad_signal, part_first, part_second)


def solution(mesh):
    placed = (
        P("batch", "seq", None),
        P(),
        P("seq", None, None),
        P("seq", None, None),
        P("batch", "seq", None),
    )
    return jax.shard_map(
        body,
        mesh=mesh,
        in_specs=placed,
        out_specs=(P("batch", "seq", None), P("seq", "batch", None), P("seq", "batch", None)),
        check_vma=False,
    )
```

```python
import jax
import jax.numpy as jnp
from jax import lax
from jax.sharding import PartitionSpec as P
from jax.experimental import pallas as pl
from jax.experimental.pallas import tpu as pltpu


def _grad_payload_kernel(s_ref, g_ref, o_ref, product):
    peers, group, _ = o_ref.shape
    width = g_ref.shape[-1]
    lanes = product.shape[-1]
    for k in range(s_ref.shape[0]):
        full = lax.dot_general(
            s_ref[k], g_ref[k], (((0,), (0,)), ((), ())), preferred_element_type=jnp.float32
        )
        for c in range(width // lanes):
            product[c] = full[:, c * lanes : (c + 1) * lanes]
        for i in range(group):
            for c in range(width // lanes):
                rows = product[c, pl.ds(i, peers, stride=group), :]
                start = k * width + c * lanes
                o_ref[:, i, start : start + lanes] = rows.astype(o_ref.dtype)


def grad_payload(second_factor, upstream, peers):
    col_blocks, rows, order = second_factor.shape
    width = upstream.shape[-1]
    flops = 2 * col_blocks * rows * order * width
    return pl.pallas_call(
        _grad_payload_kernel,
        out_shape=jax.ShapeDtypeStruct((peers, order // peers, col_blocks * width), jnp.bfloat16),
        in_specs=[pl.BlockSpec(memory_space=pltpu.VMEM)] * 2,
        out_specs=pl.BlockSpec(memory_space=pltpu.VMEM),
        scratch_shapes=[pltpu.VMEM((width // 128, order, 128), jnp.float32)],
        cost_estimate=pl.CostEstimate(
            flops=flops, transcendentals=0, bytes_accessed=2 * (second_factor.size + 2 * upstream.size)
        ),
    )(second_factor, upstream.reshape(col_blocks, rows, width))


def passed_along(value, axis, steps):
    count = lax.axis_size(axis)
    initial, last = (max(0, -steps), min(count, count - steps))
    return lax.ppermute(value, axis, [(source, source + steps) for source in range(initial, last)])


def body(signal, conv_weight, first_factor, second_factor, grad_output):
    seq_count, tok_rows, channels = signal.shape
    blocks = first_factor.shape[0]
    block_order = first_factor.shape[1]
    col_blocks = second_factor.shape[0]
    block_count = second_factor.shape[1]
    tap_count = conv_weight.shape[0]
    peers = lax.axis_size("seq")
    previous = passed_along(signal[:, tok_rows - (tap_count - 1) :, :], "seq", 1)
    padded_in = jnp.concatenate([previous, signal], axis=1).astype(jnp.float32)
    conv_out = sum(
        (
            conv_weight[r][None, None, :]
            * padded_in[:, tap_count - 1 - r : tap_count - 1 - r + tok_rows, :]
            for r in range(tap_count)
        )
    )
    gate_val = jax.nn.sigmoid(conv_out)
    hidden = (conv_out * gate_val).astype(jnp.bfloat16)
    hidden_blocks = hidden.reshape(seq_count, blocks, block_order, channels)
    first_split = first_factor.reshape(blocks, peers, col_blocks, block_order)
    mixed_chunks = jnp.einsum(
        "ipqj,sijd->psiqd", first_split, hidden_blocks, preferred_element_type=jnp.float32
    ).astype(jnp.bfloat16)
    upstream = grad_output.reshape(seq_count, col_blocks, block_count, channels)
    grad_chunks = grad_payload(second_factor, upstream, peers)
    grad_rows = lax.all_to_all(grad_chunks, "seq", split_axis=0, concat_axis=0, tiled=True).reshape(
        peers, seq_count, blocks, col_blocks, channels
    )
    columns = lax.all_to_all(mixed_chunks, "seq", split_axis=0, concat_axis=0, tiled=True)
    halves = lax.axis_size("batch")
    me = lax.axis_index("batch")
    other = halves - 1 - me
    rows_half = block_count // halves
    peers_half = peers // halves

    def second_part(half):
        up = lax.dynamic_slice_in_dim(upstream, half * rows_half, rows_half, 2)
        return jnp.einsum(
            "skmd,psikd->kmpi", up, columns, preferred_element_type=jnp.float32
        ).reshape(col_blocks, rows_half, peers * blocks).astype(jnp.bfloat16)

    def first_part(half):
        gr = lax.dynamic_slice_in_dim(grad_rows, half * peers_half, peers_half, 0)
        return jnp.einsum(
            "psiqd,sijd->ipqj", gr, hidden_blocks, preferred_element_type=jnp.float32
        ).reshape(blocks, peers_half * col_blocks, block_order).astype(jnp.bfloat16)

    swap = [(0, 1), (1, 0)]
    sent_second = lax.ppermute(second_part(other), "batch", swap)
    sent_first = lax.ppermute(first_part(other), "batch", swap)
    grad_hidden = jnp.einsum(
        "ipqj,psiqd->sijd", first_split, grad_rows, preferred_element_type=jnp.float32
    ).reshape(seq_count, tok_rows, channels)
    part_second = (
        second_part(me).astype(jnp.float32) + sent_second.astype(jnp.float32)
    ).astype(jnp.bfloat16)
    part_first = (
        first_part(me).astype(jnp.float32) + sent_first.astype(jnp.float32)
    ).astype(jnp.bfloat16)
    grad_conv = (grad_hidden * gate_val * (1.0 + conv_out * (1.0 - gate_val))).astype(jnp.bfloat16)
    following = passed_along(grad_conv[:, : tap_count - 1, :], "seq", -1)
    extended = jnp.concatenate([grad_conv, following], axis=1).astype(jnp.float32)
    grad_signal = sum(
        (conv_weight[r][None, None, :] * extended[:, r : r + tok_rows, :] for r in range(tap_count))
    ).astype(jnp.bfloat16)
    return (grad_signal, part_first, part_second)


def solution(mesh):
    placed = (
        P("batch", "seq", None),
        P(),
        P("seq", None, None),
        P("seq", None, None),
        P("batch", "seq", None),
    )
    return jax.shard_map(
        body,
        mesh=mesh,
        in_specs=placed,
        out_specs=(P("batch", "seq", None), P("seq", "batch", None), P("seq", "batch", None)),
        check_vma=False,
    )
```

```python
import jax
import jax.numpy as jnp
from jax import lax
from jax.sharding import PartitionSpec as P
from jax.experimental import pallas as pl
from jax.experimental.pallas import tpu as pltpu


def _grad_payload_kernel(s_ref, g_ref, o_ref):
    product = lax.dot_general(
        s_ref[0], g_ref[0], (((0,), (0,)), ((), ())), preferred_element_type=jnp.float32
    )
    o_ref[...] = product.astype(o_ref.dtype)


def grad_payload(second_factor, upstream):
    col_blocks, rows, order = second_factor.shape
    width = upstream.shape[-1]
    flops = 2 * col_blocks * rows * order * width
    return pl.pallas_call(
        _grad_payload_kernel,
        grid=(col_blocks,),
        out_shape=jax.ShapeDtypeStruct((order, col_blocks * width), jnp.bfloat16),
        in_specs=[
            pl.BlockSpec((1, rows, order), lambda k: (k, 0, 0)),
            pl.BlockSpec((1, rows, width), lambda k: (k, 0, 0)),
        ],
        out_specs=pl.BlockSpec((order, width), lambda k: (0, k)),
        cost_estimate=pl.CostEstimate(
            flops=flops, transcendentals=0, bytes_accessed=2 * (second_factor.size + 2 * upstream.size)
        ),
    )(second_factor, upstream.reshape(col_blocks, rows, width))


def passed_along(value, axis, steps):
    count = lax.axis_size(axis)
    initial, last = (max(0, -steps), min(count, count - steps))
    return lax.ppermute(value, axis, [(source, source + steps) for source in range(initial, last)])


def body(signal, conv_weight, first_factor, second_factor, grad_output):
    seq_count, tok_rows, channels = signal.shape
    blocks = first_factor.shape[0]
    block_order = first_factor.shape[1]
    col_blocks = second_factor.shape[0]
    block_count = second_factor.shape[1]
    tap_count = conv_weight.shape[0]
    peers = lax.axis_size("seq")
    previous = passed_along(signal[:, tok_rows - (tap_count - 1) :, :], "seq", 1)
    padded_in = jnp.concatenate([previous, signal], axis=1).astype(jnp.float32)
    conv_out = sum(
        (
            conv_weight[r][None, None, :]
            * padded_in[:, tap_count - 1 - r : tap_count - 1 - r + tok_rows, :]
            for r in range(tap_count)
        )
    )
    gate_val = jax.nn.sigmoid(conv_out)
    hidden = (conv_out * gate_val).astype(jnp.bfloat16)
    hidden_blocks = hidden.reshape(seq_count, blocks, block_order, channels)
    first_split = first_factor.reshape(blocks, peers, col_blocks, block_order)
    mixed_chunks = jnp.einsum(
        "ipqj,sijd->psiqd", first_split, hidden_blocks, preferred_element_type=jnp.float32
    ).astype(jnp.bfloat16)
    upstream = grad_output.reshape(seq_count, col_blocks, block_count, channels)
    grad_chunks = grad_payload(second_factor, upstream).reshape(
        peers, seq_count, blocks, col_blocks, channels
    )
    grad_rows = lax.all_to_all(grad_chunks, "seq", split_axis=0, concat_axis=0, tiled=True)
    columns = lax.all_to_all(mixed_chunks, "seq", split_axis=0, concat_axis=0, tiled=True)
    halves = lax.axis_size("batch")
    me = lax.axis_index("batch")
    other = halves - 1 - me
    rows_half = block_count // halves
    peers_half = peers // halves

    def second_part(half):
        up = lax.dynamic_slice_in_dim(upstream, half * rows_half, rows_half, 2)
        return jnp.einsum(
            "skmd,psikd->kmpi", up, columns, preferred_element_type=jnp.float32
        ).reshape(col_blocks, rows_half, peers * blocks).astype(jnp.bfloat16)

    def first_part(half):
        gr = lax.dynamic_slice_in_dim(grad_rows, half * peers_half, peers_half, 0)
        return jnp.einsum(
            "psiqd,sijd->ipqj", gr, hidden_blocks, preferred_element_type=jnp.float32
        ).reshape(blocks, peers_half * col_blocks, block_order).astype(jnp.bfloat16)

    swap = [(0, 1), (1, 0)]
    sent_second = lax.ppermute(second_part(other), "batch", swap)
    sent_first = lax.ppermute(first_part(other), "batch", swap)
    grad_hidden = jnp.einsum(
        "ipqj,psiqd->sijd", first_split, grad_rows, preferred_element_type=jnp.float32
    ).reshape(seq_count, tok_rows, channels)
    part_second = (
        second_part(me).astype(jnp.float32) + sent_second.astype(jnp.float32)
    ).astype(jnp.bfloat16)
    part_first = (
        first_part(me).astype(jnp.float32) + sent_first.astype(jnp.float32)
    ).astype(jnp.bfloat16)
    grad_conv = (grad_hidden * gate_val * (1.0 + conv_out * (1.0 - gate_val))).astype(jnp.bfloat16)
    following = passed_along(grad_conv[:, : tap_count - 1, :], "seq", -1)
    extended = jnp.concatenate([grad_conv, following], axis=1).astype(jnp.float32)
    grad_signal = sum(
        (conv_weight[r][None, None, :] * extended[:, r : r + tok_rows, :] for r in range(tap_count))
    ).astype(jnp.bfloat16)
    return (grad_signal, part_first, part_second)


def solution(mesh):
    placed = (
        P("batch", "seq", None),
        P(),
        P("seq", None, None),
        P("seq", None, None),
        P("batch", "seq", None),
    )
    return jax.shard_map(
        body,
        mesh=mesh,
        in_specs=placed,
        out_specs=(P("batch", "seq", None), P("seq", "batch", None), P("seq", "batch", None)),
        check_vma=False,
    )
```

```python
import jax
import jax.numpy as jnp
from jax import lax
from jax.sharding import PartitionSpec as P
from jax.experimental import pallas as pl
from jax.experimental.pallas import tpu as pltpu


def _grad_payload_kernel(s_ref, g_ref, o_ref):
    width = g_ref.shape[-1]
    for k in range(s_ref.shape[0]):
        product = lax.dot_general(
            s_ref[k], g_ref[k], (((0,), (0,)), ((), ())), preferred_element_type=jnp.float32
        )
        o_ref[:, k * width : (k + 1) * width] = product.astype(o_ref.dtype)


def grad_payload(second_factor, upstream):
    col_blocks, rows, order = second_factor.shape
    width = upstream.shape[-1]
    flops = 2 * col_blocks * rows * order * width
    return pl.pallas_call(
        _grad_payload_kernel,
        out_shape=jax.ShapeDtypeStruct((order, col_blocks * width), jnp.bfloat16),
        in_specs=[pl.BlockSpec(memory_space=pltpu.VMEM)] * 2,
        out_specs=pl.BlockSpec(memory_space=pltpu.VMEM),
        cost_estimate=pl.CostEstimate(
            flops=flops, transcendentals=0, bytes_accessed=2 * (second_factor.size + 2 * upstream.size)
        ),
    )(second_factor, upstream.reshape(col_blocks, rows, width))


def passed_along(value, axis, steps):
    count = lax.axis_size(axis)
    initial, last = (max(0, -steps), min(count, count - steps))
    return lax.ppermute(value, axis, [(source, source + steps) for source in range(initial, last)])


def body(signal, conv_weight, first_factor, second_factor, grad_output):
    seq_count, tok_rows, channels = signal.shape
    blocks = first_factor.shape[0]
    block_order = first_factor.shape[1]
    col_blocks = second_factor.shape[0]
    block_count = second_factor.shape[1]
    tap_count = conv_weight.shape[0]
    peers = lax.axis_size("seq")
    previous = passed_along(signal[:, tok_rows - (tap_count - 1) :, :], "seq", 1)
    padded_in = jnp.concatenate([previous, signal], axis=1).astype(jnp.float32)
    conv_out = sum(
        (
            conv_weight[r][None, None, :]
            * padded_in[:, tap_count - 1 - r : tap_count - 1 - r + tok_rows, :]
            for r in range(tap_count)
        )
    )
    gate_val = jax.nn.sigmoid(conv_out)
    hidden = (conv_out * gate_val).astype(jnp.bfloat16)
    hidden_blocks = hidden.reshape(seq_count, blocks, block_order, channels)
    first_split = first_factor.reshape(blocks, peers, col_blocks, block_order)
    mixed_chunks = jnp.einsum(
        "ipqj,sijd->psqid", first_split, hidden_blocks, preferred_element_type=jnp.float32
    ).astype(jnp.bfloat16)
    upstream = grad_output.reshape(seq_count, col_blocks, block_count, channels)
    grad_chunks = grad_payload(second_factor, upstream).reshape(
        peers, seq_count, blocks, col_blocks, channels
    )
    grad_rows = lax.all_to_all(grad_chunks, "seq", split_axis=0, concat_axis=0, tiled=True)
    columns = lax.all_to_all(mixed_chunks, "seq", split_axis=0, concat_axis=3, tiled=True)[0]
    halves = lax.axis_size("batch")
    me = lax.axis_index("batch")
    other = halves - 1 - me
    rows_half = block_count // halves
    peers_half = peers // halves

    def second_part(half):
        up = lax.dynamic_slice_in_dim(upstream, half * rows_half, rows_half, 2)
        return jnp.einsum(
            "skmd,skid->kmi", up, columns, preferred_element_type=jnp.float32
        ).astype(jnp.bfloat16)

    def first_part(half):
        gr = lax.dynamic_slice_in_dim(grad_rows, half * peers_half, peers_half, 0)
        return jnp.einsum(
            "psiqd,sijd->ipqj", gr, hidden_blocks, preferred_element_type=jnp.float32
        ).reshape(blocks, peers_half * col_blocks, block_order).astype(jnp.bfloat16)

    swap = [(0, 1), (1, 0)]
    sent_second = lax.ppermute(second_part(other), "batch", swap)
    sent_first = lax.ppermute(first_part(other), "batch", swap)
    grad_hidden = jnp.einsum(
        "ipqj,psiqd->sijd", first_split, grad_rows, preferred_element_type=jnp.float32
    ).reshape(seq_count, tok_rows, channels)
    part_second = (
        second_part(me).astype(jnp.float32) + sent_second.astype(jnp.float32)
    ).astype(jnp.bfloat16)
    part_first = (
        first_part(me).astype(jnp.float32) + sent_first.astype(jnp.float32)
    ).astype(jnp.bfloat16)
    grad_conv = (grad_hidden * gate_val * (1.0 + conv_out * (1.0 - gate_val))).astype(jnp.bfloat16)
    following = passed_along(grad_conv[:, : tap_count - 1, :], "seq", -1)
    extended = jnp.concatenate([grad_conv, following], axis=1).astype(jnp.float32)
    grad_signal = sum(
        (conv_weight[r][None, None, :] * extended[:, r : r + tok_rows, :] for r in range(tap_count))
    ).astype(jnp.bfloat16)
    return (grad_signal, part_first, part_second)


def solution(mesh):
    placed = (
        P("batch", "seq", None),
        P(),
        P("seq", None, None),
        P("seq", None, None),
        P("batch", "seq", None),
    )
    return jax.shard_map(
        body,
        mesh=mesh,
        in_specs=placed,
        out_specs=(P("batch", "seq", None), P("seq", "batch", None), P("seq", "batch", None)),
        check_vma=False,
    )
```

```python
import jax
import jax.numpy as jnp
from jax import lax
from jax.sharding import PartitionSpec as P
from jax.experimental import pallas as pl
from jax.experimental.pallas import tpu as pltpu


def _grad_payload_kernel(s_ref, g_ref, o_ref):
    width = g_ref.shape[-1]
    for k in range(s_ref.shape[0]):
        product = lax.dot_general(
            s_ref[k], g_ref[k], (((0,), (0,)), ((), ())), preferred_element_type=jnp.float32
        )
        o_ref[:, k * width : (k + 1) * width] = product.astype(o_ref.dtype)


def grad_payload(second_factor, upstream):
    col_blocks, rows, order = second_factor.shape
    width = upstream.shape[-1]
    flops = 2 * col_blocks * rows * order * width
    return pl.pallas_call(
        _grad_payload_kernel,
        out_shape=jax.ShapeDtypeStruct((order, col_blocks * width), jnp.bfloat16),
        in_specs=[pl.BlockSpec(memory_space=pltpu.VMEM)] * 2,
        out_specs=pl.BlockSpec(memory_space=pltpu.VMEM),
        cost_estimate=pl.CostEstimate(
            flops=flops, transcendentals=0, bytes_accessed=2 * (second_factor.size + 2 * upstream.size)
        ),
    )(second_factor, upstream.reshape(col_blocks, rows, width))


def passed_along(value, axis, steps):
    count = lax.axis_size(axis)
    initial, last = (max(0, -steps), min(count, count - steps))
    return lax.ppermute(value, axis, [(source, source + steps) for source in range(initial, last)])


def body(signal, conv_weight, first_factor, second_factor, grad_output):
    seq_count, tok_rows, channels = signal.shape
    blocks = first_factor.shape[0]
    block_order = first_factor.shape[1]
    col_blocks = second_factor.shape[0]
    block_count = second_factor.shape[1]
    tap_count = conv_weight.shape[0]
    peers = lax.axis_size("seq")
    previous = passed_along(signal[:, tok_rows - (tap_count - 1) :, :], "seq", 1)
    padded_in = jnp.concatenate([previous, signal], axis=1).astype(jnp.float32)
    conv_out = sum(
        (
            conv_weight[r][None, None, :]
            * padded_in[:, tap_count - 1 - r : tap_count - 1 - r + tok_rows, :]
            for r in range(tap_count)
        )
    )
    gate_val = jax.nn.sigmoid(conv_out)
    hidden = (conv_out * gate_val).astype(jnp.bfloat16)
    hidden_blocks = hidden.reshape(seq_count, blocks, block_order, channels)
    first_split = first_factor.reshape(blocks, peers, col_blocks, block_order)
    mixed_chunks = jnp.einsum(
        "ipqj,sijd->psiqd", first_split, hidden_blocks, preferred_element_type=jnp.float32
    ).astype(jnp.bfloat16)
    upstream = grad_output.reshape(seq_count, col_blocks, block_count, channels)
    grad_chunks = grad_payload(second_factor, upstream).reshape(
        peers, seq_count, blocks, col_blocks, channels
    )
    grad_rows = lax.all_to_all(grad_chunks, "seq", split_axis=0, concat_axis=0, tiled=True)
    columns = lax.all_to_all(mixed_chunks, "seq", split_axis=0, concat_axis=0, tiled=True)
    halves = lax.axis_size("batch")
    me = lax.axis_index("batch")
    other = halves - 1 - me
    rows_half = block_count // halves
    peers_half = peers // halves

    def second_part(half):
        up = lax.dynamic_slice_in_dim(upstream, half * rows_half, rows_half, 2)
        return jnp.einsum(
            "skmd,psikd->kmpi", up, columns, preferred_element_type=jnp.float32
        ).reshape(col_blocks, rows_half, peers * blocks).astype(jnp.bfloat16)

    def first_part(half):
        gr = lax.dynamic_slice_in_dim(grad_rows, half * peers_half, peers_half, 0)
        return jnp.einsum(
            "psiqd,sijd->ipqj", gr, hidden_blocks, preferred_element_type=jnp.float32
        ).reshape(blocks, peers_half * col_blocks, block_order).astype(jnp.bfloat16)

    swap = [(0, 1), (1, 0)]
    sent_second = lax.ppermute(second_part(other), "batch", swap)
    sent_first = lax.ppermute(first_part(other), "batch", swap)
    grad_hidden = jnp.einsum(
        "ipqj,psiqd->sijd", first_split, grad_rows, preferred_element_type=jnp.float32
    ).reshape(seq_count, tok_rows, channels)
    kept = lambda part: lax.reduce_precision(part.astype(jnp.float32), exponent_bits=8, mantissa_bits=7)
    part_second = (kept(second_part(me)) + sent_second.astype(jnp.float32)).astype(jnp.bfloat16)
    part_first = (kept(first_part(me)) + sent_first.astype(jnp.float32)).astype(jnp.bfloat16)
    grad_conv = (grad_hidden * gate_val * (1.0 + conv_out * (1.0 - gate_val))).astype(jnp.bfloat16)
    following = passed_along(grad_conv[:, : tap_count - 1, :], "seq", -1)
    extended = jnp.concatenate([grad_conv, following], axis=1).astype(jnp.float32)
    grad_signal = sum(
        (conv_weight[r][None, None, :] * extended[:, r : r + tok_rows, :] for r in range(tap_count))
    ).astype(jnp.bfloat16)
    return (grad_signal, part_first, part_second)


def solution(mesh):
    placed = (
        P("batch", "seq", None),
        P(),
        P("seq", None, None),
        P("seq", None, None),
        P("batch", "seq", None),
    )
    return jax.shard_map(
        body,
        mesh=mesh,
        in_specs=placed,
        out_specs=(P("batch", "seq", None), P("seq", "batch", None), P("seq", "batch", None)),
        check_vma=False,
    )
```

```python
import jax
import jax.numpy as jnp
from jax import lax
from jax.sharding import PartitionSpec as P
from jax.experimental import pallas as pl
from jax.experimental.pallas import tpu as pltpu


def _grad_payload_kernel(s_ref, g_ref, o_ref):
    width = g_ref.shape[-1]
    for k in range(s_ref.shape[0]):
        product = lax.dot_general(
            s_ref[k], g_ref[k], (((0,), (0,)), ((), ())), preferred_element_type=jnp.float32
        )
        o_ref[:, k * width : (k + 1) * width] = product.astype(o_ref.dtype)


def grad_payload(second_factor, upstream):
    col_blocks, rows, order = second_factor.shape
    width = upstream.shape[-1]
    flops = 2 * col_blocks * rows * order * width
    return pl.pallas_call(
        _grad_payload_kernel,
        out_shape=jax.ShapeDtypeStruct((order, col_blocks * width), jnp.bfloat16),
        in_specs=[pl.BlockSpec(memory_space=pltpu.VMEM)] * 2,
        out_specs=pl.BlockSpec(memory_space=pltpu.VMEM),
        cost_estimate=pl.CostEstimate(
            flops=flops, transcendentals=0, bytes_accessed=2 * (second_factor.size + 2 * upstream.size)
        ),
    )(second_factor, upstream.reshape(col_blocks, rows, width))


def passed_along(value, axis, steps):
    count = lax.axis_size(axis)
    initial, last = (max(0, -steps), min(count, count - steps))
    return lax.ppermute(value, axis, [(source, source + steps) for source in range(initial, last)])


def body(signal, conv_weight, first_factor, second_factor, grad_output):
    seq_count, tok_rows, channels = signal.shape
    blocks = first_factor.shape[0]
    block_order = first_factor.shape[1]
    col_blocks = second_factor.shape[0]
    block_count = second_factor.shape[1]
    tap_count = conv_weight.shape[0]
    peers = lax.axis_size("seq")
    previous = passed_along(signal[:, tok_rows - (tap_count - 1) :, :], "seq", 1)
    padded_in = jnp.concatenate([previous, signal], axis=1).astype(jnp.float32)
    conv_out = sum(
        (
            conv_weight[r][None, None, :]
            * padded_in[:, tap_count - 1 - r : tap_count - 1 - r + tok_rows, :]
            for r in range(tap_count)
        )
    )
    gate_val = jax.nn.sigmoid(conv_out)
    hidden = (conv_out * gate_val).astype(jnp.bfloat16)
    hidden_blocks = hidden.reshape(seq_count, blocks, block_order, channels)
    first_split = first_factor.reshape(blocks, peers, col_blocks, block_order)
    mixed_chunks = jnp.einsum(
        "ipqj,sijd->psqid", first_split, hidden_blocks, preferred_element_type=jnp.float32
    ).astype(jnp.bfloat16)
    upstream = grad_output.reshape(seq_count, col_blocks, block_count, channels)
    grad_chunks = grad_payload(second_factor, upstream).reshape(
        peers, seq_count, blocks, col_blocks, channels
    )
    grad_rows = lax.all_to_all(grad_chunks, "seq", split_axis=0, concat_axis=0, tiled=True)
    columns = lax.all_to_all(mixed_chunks, "seq", split_axis=0, concat_axis=3, tiled=True)[0]
    halves = lax.axis_size("batch")
    me = lax.axis_index("batch")
    other = halves - 1 - me
    rows_half = block_count // halves
    peers_half = peers // halves

    def second_part(half):
        up = lax.dynamic_slice_in_dim(upstream, half * rows_half, rows_half, 2)
        return jnp.einsum(
            "skmd,skid->kmi", up, columns, preferred_element_type=jnp.float32
        ).astype(jnp.bfloat16)

    def first_part(half):
        gr = lax.dynamic_slice_in_dim(grad_rows, half * peers_half, peers_half, 0)
        return jnp.einsum(
            "psiqd,sijd->ipqj", gr, hidden_blocks, preferred_element_type=jnp.float32
        ).reshape(blocks, peers_half * col_blocks, block_order).astype(jnp.bfloat16)

    swap = [(0, 1), (1, 0)]
    sent_second = lax.ppermute(second_part(other), "batch", swap)
    sent_first = lax.ppermute(first_part(other), "batch", swap)
    grad_hidden = jnp.einsum(
        "ipqj,psiqd->sijd", first_split, grad_rows, preferred_element_type=jnp.float32
    ).reshape(seq_count, tok_rows, channels)
    kept = lambda part: lax.reduce_precision(part.astype(jnp.float32), exponent_bits=8, mantissa_bits=7)
    own_second = lax.optimization_barrier(kept(second_part(me)))
    part_second = (own_second + sent_second.astype(jnp.float32)).astype(jnp.bfloat16)
    part_first = (kept(first_part(me)) + sent_first.astype(jnp.float32)).astype(jnp.bfloat16)
    grad_conv = (grad_hidden * gate_val * (1.0 + conv_out * (1.0 - gate_val))).astype(jnp.bfloat16)
    following = passed_along(grad_conv[:, : tap_count - 1, :], "seq", -1)
    extended = jnp.concatenate([grad_conv, following], axis=1).astype(jnp.float32)
    grad_signal = sum(
        (conv_weight[r][None, None, :] * extended[:, r : r + tok_rows, :] for r in range(tap_count))
    ).astype(jnp.bfloat16)
    return (grad_signal, part_first, part_second)


def solution(mesh):
    placed = (
        P("batch", "seq", None),
        P(),
        P("seq", None, None),
        P("seq", None, None),
        P("batch", "seq", None),
    )
    return jax.shard_map(
        body,
        mesh=mesh,
        in_specs=placed,
        out_specs=(P("batch", "seq", None), P("seq", "batch", None), P("seq", "batch", None)),
        check_vma=False,
    )
```

```python
import jax
import jax.numpy as jnp
from jax import lax
from jax.sharding import PartitionSpec as P
from jax.experimental import pallas as pl
from jax.experimental.pallas import tpu as pltpu


def _grad_payload_kernel(s_ref, g_ref, o_ref):
    peers, group, _ = o_ref.shape
    width = g_ref.shape[-1]
    for k in range(s_ref.shape[0]):
        product = lax.dot_general(
            s_ref[k], g_ref[k], (((0,), (0,)), ((), ())), preferred_element_type=jnp.float32
        )
        o_ref[:, :, k * width : (k + 1) * width] = product.reshape(peers, group, width).astype(o_ref.dtype)


def grad_payload(second_factor, upstream, peers):
    col_blocks, rows, order = second_factor.shape
    width = upstream.shape[-1]
    flops = 2 * col_blocks * rows * order * width
    return pl.pallas_call(
        _grad_payload_kernel,
        out_shape=jax.ShapeDtypeStruct((peers, order // peers, col_blocks * width), jnp.bfloat16),
        in_specs=[pl.BlockSpec(memory_space=pltpu.VMEM)] * 2,
        out_specs=pl.BlockSpec(memory_space=pltpu.VMEM),
        cost_estimate=pl.CostEstimate(
            flops=flops, transcendentals=0, bytes_accessed=2 * (second_factor.size + 2 * upstream.size)
        ),
    )(second_factor, upstream.reshape(col_blocks, rows, width))


def passed_along(value, axis, steps):
    count = lax.axis_size(axis)
    initial, last = (max(0, -steps), min(count, count - steps))
    return lax.ppermute(value, axis, [(source, source + steps) for source in range(initial, last)])


def body(signal, conv_weight, first_factor, second_factor, grad_output):
    seq_count, tok_rows, channels = signal.shape
    blocks = first_factor.shape[0]
    block_order = first_factor.shape[1]
    col_blocks = second_factor.shape[0]
    block_count = second_factor.shape[1]
    tap_count = conv_weight.shape[0]
    peers = lax.axis_size("seq")
    previous = passed_along(signal[:, tok_rows - (tap_count - 1) :, :], "seq", 1)
    padded_in = jnp.concatenate([previous, signal], axis=1).astype(jnp.float32)
    conv_out = sum(
        (
            conv_weight[r][None, None, :]
            * padded_in[:, tap_count - 1 - r : tap_count - 1 - r + tok_rows, :]
            for r in range(tap_count)
        )
    )
    gate_val = jax.nn.sigmoid(conv_out)
    hidden = (conv_out * gate_val).astype(jnp.bfloat16)
    hidden_blocks = hidden.reshape(seq_count, blocks, block_order, channels)
    first_split = first_factor.reshape(blocks, peers, col_blocks, block_order)
    mixed_chunks = jnp.einsum(
        "ipqj,sijd->psqid", first_split, hidden_blocks, preferred_element_type=jnp.float32
    ).astype(jnp.bfloat16)
    upstream = grad_output.reshape(seq_count, col_blocks, block_count, channels)
    grad_chunks = grad_payload(second_factor, upstream, peers)
    grad_rows = lax.all_to_all(grad_chunks, "seq", split_axis=0, concat_axis=0, tiled=True).reshape(
        peers, seq_count, blocks, col_blocks, channels
    )
    columns = lax.all_to_all(mixed_chunks, "seq", split_axis=0, concat_axis=3, tiled=True)[0]
    halves = lax.axis_size("batch")
    me = lax.axis_index("batch")
    other = halves - 1 - me
    rows_half = block_count // halves
    peers_half = peers // halves

    def second_part(half):
        up = lax.dynamic_slice_in_dim(upstream, half * rows_half, rows_half, 2)
        return jnp.einsum(
            "skmd,skid->kmi", up, columns, preferred_element_type=jnp.float32
        ).astype(jnp.bfloat16)

    def first_part(half):
        gr = lax.dynamic_slice_in_dim(grad_rows, half * peers_half, peers_half, 0)
        return jnp.einsum(
            "psiqd,sijd->ipqj", gr, hidden_blocks, preferred_element_type=jnp.float32
        ).reshape(blocks, peers_half * col_blocks, block_order).astype(jnp.bfloat16)

    swap = [(0, 1), (1, 0)]
    sent_second = lax.ppermute(second_part(other), "batch", swap)
    sent_first = lax.ppermute(first_part(other), "batch", swap)
    grad_hidden = jnp.einsum(
        "ipqj,psiqd->sijd", first_split, grad_rows, preferred_element_type=jnp.float32
    ).reshape(seq_count, tok_rows, channels)
    kept = lambda part: lax.reduce_precision(part.astype(jnp.float32), exponent_bits=8, mantissa_bits=7)
    own_second = lax.optimization_barrier(kept(second_part(me)))
    part_second = (own_second + sent_second.astype(jnp.float32)).astype(jnp.bfloat16)
    part_first = (kept(first_part(me)) + sent_first.astype(jnp.float32)).astype(jnp.bfloat16)
    grad_conv = (grad_hidden * gate_val * (1.0 + conv_out * (1.0 - gate_val))).astype(jnp.bfloat16)
    following = passed_along(grad_conv[:, : tap_count - 1, :], "seq", -1)
    extended = jnp.concatenate([grad_conv, following], axis=1).astype(jnp.float32)
    grad_signal = sum(
        (conv_weight[r][None, None, :] * extended[:, r : r + tok_rows, :] for r in range(tap_count))
    ).astype(jnp.bfloat16)
    return (grad_signal, part_first, part_second)


def solution(mesh):
    placed = (
        P("batch", "seq", None),
        P(),
        P("seq", None, None),
        P("seq", None, None),
        P("batch", "seq", None),
    )
    return jax.shard_map(
        body,
        mesh=mesh,
        in_specs=placed,
        out_specs=(P("batch", "seq", None), P("seq", "batch", None), P("seq", "batch", None)),
        check_vma=False,
    )
```

```python
import jax
import jax.numpy as jnp
from jax import lax
from jax.sharding import PartitionSpec as P
from jax.experimental import pallas as pl
from jax.experimental.pallas import tpu as pltpu


def _grad_payload_kernel(s_ref, g_ref, o_ref):
    peers, group, _ = o_ref.shape
    width = g_ref.shape[-1]
    for k in range(s_ref.shape[0]):
        product = lax.dot_general(
            s_ref[k], g_ref[k], (((0,), (0,)), ((), ())), preferred_element_type=jnp.float32
        )
        o_ref[:, :, k * width : (k + 1) * width] = product.reshape(peers, group, width).astype(o_ref.dtype)


def grad_payload(second_factor, upstream, peers):
    col_blocks, rows, order = second_factor.shape
    width = upstream.shape[-1]
    flops = 2 * col_blocks * rows * order * width
    return pl.pallas_call(
        _grad_payload_kernel,
        out_shape=jax.ShapeDtypeStruct((peers, order // peers, col_blocks * width), jnp.bfloat16),
        in_specs=[pl.BlockSpec(memory_space=pltpu.VMEM)] * 2,
        out_specs=pl.BlockSpec(memory_space=pltpu.VMEM),
        cost_estimate=pl.CostEstimate(
            flops=flops, transcendentals=0, bytes_accessed=2 * (second_factor.size + 2 * upstream.size)
        ),
    )(second_factor, upstream.reshape(col_blocks, rows, width))


def _second_half_kernel(half_ref, up_ref, col_ref, o_ref):
    o_ref[0] = lax.dot_general(
        up_ref[0], col_ref[0], (((1,), (1,)), ((), ())), preferred_element_type=jnp.float32
    ).astype(o_ref.dtype)


def second_half(half, upstream, columns):
    col_blocks, rows, width = upstream.shape
    order = columns.shape[1]
    rows_half = rows // 2
    return pl.pallas_call(
        _second_half_kernel,
        grid_spec=pltpu.PrefetchScalarGridSpec(
            num_scalar_prefetch=1,
            grid=(col_blocks,),
            in_specs=[
                pl.BlockSpec((1, rows_half, width), lambda q, h: (q, h[0], 0)),
                pl.BlockSpec((1, order, width), lambda q, h: (q, 0, 0)),
            ],
            out_specs=pl.BlockSpec((1, rows_half, order), lambda q, h: (q, 0, 0)),
        ),
        out_shape=jax.ShapeDtypeStruct((col_blocks, rows_half, order), jnp.bfloat16),
        cost_estimate=pl.CostEstimate(
            flops=2 * col_blocks * rows_half * order * width,
            transcendentals=0,
            bytes_accessed=2 * (col_blocks * rows_half * width + columns.size + col_blocks * rows_half * order),
        ),
    )(jnp.reshape(half, (1,)).astype(jnp.int32), upstream, columns)


def passed_along(value, axis, steps):
    count = lax.axis_size(axis)
    initial, last = (max(0, -steps), min(count, count - steps))
    return lax.ppermute(value, axis, [(source, source + steps) for source in range(initial, last)])


def body(signal, conv_weight, first_factor, second_factor, grad_output):
    seq_count, tok_rows, channels = signal.shape
    blocks = first_factor.shape[0]
    block_order = first_factor.shape[1]
    col_blocks = second_factor.shape[0]
    block_count = second_factor.shape[1]
    tap_count = conv_weight.shape[0]
    peers = lax.axis_size("seq")
    previous = passed_along(signal[:, tok_rows - (tap_count - 1) :, :], "seq", 1)
    padded_in = jnp.concatenate([previous, signal], axis=1).astype(jnp.float32)
    conv_out = sum(
        (
            conv_weight[r][None, None, :]
            * padded_in[:, tap_count - 1 - r : tap_count - 1 - r + tok_rows, :]
            for r in range(tap_count)
        )
    )
    gate_val = jax.nn.sigmoid(conv_out)
    hidden = (conv_out * gate_val).astype(jnp.bfloat16)
    hidden_blocks = hidden.reshape(seq_count, blocks, block_order, channels)
    first_split = first_factor.reshape(blocks, peers, col_blocks, block_order)
    mixed_chunks = jnp.einsum(
        "ipqj,sijd->psqid", first_split, hidden_blocks, preferred_element_type=jnp.float32
    ).astype(jnp.bfloat16)
    upstream = grad_output.reshape(seq_count, col_blocks, block_count, channels)
    grad_chunks = grad_payload(second_factor, upstream, peers)
    grad_rows = lax.all_to_all(grad_chunks, "seq", split_axis=0, concat_axis=0, tiled=True).reshape(
        peers, seq_count, blocks, col_blocks, channels
    )
    columns = lax.all_to_all(mixed_chunks, "seq", split_axis=0, concat_axis=3, tiled=True)[0]
    halves = lax.axis_size("batch")
    me = lax.axis_index("batch")
    other = halves - 1 - me
    rows_half = block_count // halves
    peers_half = peers // halves

    def second_part(half):
        return second_half(
            half,
            upstream.reshape(col_blocks, block_count, channels),
            columns.reshape(col_blocks, peers * blocks, channels),
        )

    def first_part(half):
        gr = lax.dynamic_slice_in_dim(grad_rows, half * peers_half, peers_half, 0)
        return jnp.einsum(
            "psiqd,sijd->ipqj", gr, hidden_blocks, preferred_element_type=jnp.float32
        ).reshape(blocks, peers_half * col_blocks, block_order).astype(jnp.bfloat16)

    swap = [(0, 1), (1, 0)]
    sent_second = lax.ppermute(second_part(other), "batch", swap)
    sent_first = lax.ppermute(first_part(other), "batch", swap)
    grad_hidden = jnp.einsum(
        "ipqj,psiqd->sijd", first_split, grad_rows, preferred_element_type=jnp.float32
    ).reshape(seq_count, tok_rows, channels)
    kept = lambda part: lax.reduce_precision(part.astype(jnp.float32), exponent_bits=8, mantissa_bits=7)
    own_second = lax.optimization_barrier(kept(second_part(me)))
    part_second = (own_second + sent_second.astype(jnp.float32)).astype(jnp.bfloat16)
    part_first = (kept(first_part(me)) + sent_first.astype(jnp.float32)).astype(jnp.bfloat16)
    grad_conv = (grad_hidden * gate_val * (1.0 + conv_out * (1.0 - gate_val))).astype(jnp.bfloat16)
    following = passed_along(grad_conv[:, : tap_count - 1, :], "seq", -1)
    extended = jnp.concatenate([grad_conv, following], axis=1).astype(jnp.float32)
    grad_signal = sum(
        (conv_weight[r][None, None, :] * extended[:, r : r + tok_rows, :] for r in range(tap_count))
    ).astype(jnp.bfloat16)
    return (grad_signal, part_first, part_second)


def solution(mesh):
    placed = (
        P("batch", "seq", None),
        P(),
        P("seq", None, None),
        P("seq", None, None),
        P("batch", "seq", None),
    )
    return jax.shard_map(
        body,
        mesh=mesh,
        in_specs=placed,
        out_specs=(P("batch", "seq", None), P("seq", "batch", None), P("seq", "batch", None)),
        check_vma=False,
    )
```

```python
import jax
import jax.numpy as jnp
from jax import lax
from jax.sharding import PartitionSpec as P
from jax.experimental import pallas as pl
from jax.experimental.pallas import tpu as pltpu


def _grad_payload_kernel(s_ref, g_ref, o_ref):
    peers, group, _ = o_ref.shape
    width = g_ref.shape[-1]
    for k in range(s_ref.shape[0]):
        product = lax.dot_general(
            s_ref[k], g_ref[k], (((0,), (0,)), ((), ())), preferred_element_type=jnp.float32
        )
        o_ref[:, :, k * width : (k + 1) * width] = product.reshape(peers, group, width).astype(o_ref.dtype)


def grad_payload(second_factor, upstream, peers):
    col_blocks, rows, order = second_factor.shape
    width = upstream.shape[-1]
    flops = 2 * col_blocks * rows * order * width
    return pl.pallas_call(
        _grad_payload_kernel,
        out_shape=jax.ShapeDtypeStruct((peers, order // peers, col_blocks * width), jnp.bfloat16),
        in_specs=[pl.BlockSpec(memory_space=pltpu.VMEM)] * 2,
        out_specs=pl.BlockSpec(memory_space=pltpu.VMEM),
        cost_estimate=pl.CostEstimate(
            flops=flops, transcendentals=0, bytes_accessed=2 * (second_factor.size + 2 * upstream.size)
        ),
    )(second_factor, upstream.reshape(col_blocks, rows, width))


def passed_along(value, axis, steps):
    count = lax.axis_size(axis)
    initial, last = (max(0, -steps), min(count, count - steps))
    return lax.ppermute(value, axis, [(source, source + steps) for source in range(initial, last)])


def body(signal, conv_weight, first_factor, second_factor, grad_output):
    seq_count, tok_rows, channels = signal.shape
    blocks = first_factor.shape[0]
    block_order = first_factor.shape[1]
    col_blocks = second_factor.shape[0]
    block_count = second_factor.shape[1]
    tap_count = conv_weight.shape[0]
    peers = lax.axis_size("seq")
    previous = passed_along(signal[:, tok_rows - (tap_count - 1) :, :], "seq", 1)
    padded_in = jnp.concatenate([previous, signal], axis=1).astype(jnp.float32)
    conv_out = sum(
        (
            conv_weight[r][None, None, :]
            * padded_in[:, tap_count - 1 - r : tap_count - 1 - r + tok_rows, :]
            for r in range(tap_count)
        )
    )
    gate_val = jax.nn.sigmoid(conv_out)
    hidden = (conv_out * gate_val).astype(jnp.bfloat16)
    hidden_blocks = hidden.reshape(seq_count, blocks, block_order, channels)
    first_split = first_factor.reshape(blocks, peers, col_blocks, block_order)
    mixed_chunks = jnp.einsum(
        "ipqj,sijd->psqid", first_split, hidden_blocks, preferred_element_type=jnp.float32
    ).astype(jnp.bfloat16)
    upstream = grad_output.reshape(seq_count, col_blocks, block_count, channels)
    grad_chunks = grad_payload(second_factor, upstream, peers)
    grad_rows = lax.all_to_all(grad_chunks, "seq", split_axis=0, concat_axis=0, tiled=True).reshape(
        peers, seq_count, blocks, col_blocks, channels
    )
    columns = lax.all_to_all(mixed_chunks, "seq", split_axis=0, concat_axis=3, tiled=True)[0]
    halves = lax.axis_size("batch")
    me = lax.axis_index("batch")
    other = halves - 1 - me
    rows_half = block_count // halves
    peers_half = peers // halves

    def second_part(half):
        up = lax.dynamic_slice_in_dim(upstream, half * rows_half, rows_half, 2)
        return jnp.einsum(
            "skmd,skid->kmi", up, columns, preferred_element_type=jnp.float32
        ).astype(jnp.bfloat16)

    def first_part(half):
        gr = lax.dynamic_slice_in_dim(grad_rows, half * peers_half, peers_half, 0)
        return jnp.einsum(
            "psiqd,sijd->ipqj", gr, hidden_blocks, preferred_element_type=jnp.float32
        ).reshape(blocks, peers_half * col_blocks, block_order).astype(jnp.bfloat16)

    swap = [(0, 1), (1, 0)]
    sent_second = lax.ppermute(second_part(other), "batch", swap)
    sent_first = lax.ppermute(first_part(other), "batch", swap)
    grad_hidden = jnp.einsum(
        "ipqj,psiqd->sijd", first_split, grad_rows, preferred_element_type=jnp.float32
    ).reshape(seq_count, tok_rows, channels)
    kept = lambda part: lax.reduce_precision(part.astype(jnp.float32), exponent_bits=8, mantissa_bits=7)
    own_second = lax.optimization_barrier(kept(second_part(me)))
    part_second = (own_second + sent_second.astype(jnp.float32)).astype(jnp.bfloat16)
    rows_late, sent_first = lax.optimization_barrier((grad_rows, sent_first))
    gr_own = lax.dynamic_slice_in_dim(rows_late, me * peers_half, peers_half, 0)
    own_first = jnp.einsum(
        "psiqd,sijd->ipqj", gr_own, hidden_blocks, preferred_element_type=jnp.float32
    ).reshape(blocks, peers_half * col_blocks, block_order)
    part_first = (kept(own_first) + sent_first.astype(jnp.float32)).astype(jnp.bfloat16)
    grad_conv = (grad_hidden * gate_val * (1.0 + conv_out * (1.0 - gate_val))).astype(jnp.bfloat16)
    following = passed_along(grad_conv[:, : tap_count - 1, :], "seq", -1)
    extended = jnp.concatenate([grad_conv, following], axis=1).astype(jnp.float32)
    grad_signal = sum(
        (conv_weight[r][None, None, :] * extended[:, r : r + tok_rows, :] for r in range(tap_count))
    ).astype(jnp.bfloat16)
    return (grad_signal, part_first, part_second)


def solution(mesh):
    placed = (
        P("batch", "seq", None),
        P(),
        P("seq", None, None),
        P("seq", None, None),
        P("batch", "seq", None),
    )
    return jax.shard_map(
        body,
        mesh=mesh,
        in_specs=placed,
        out_specs=(P("batch", "seq", None), P("seq", "batch", None), P("seq", "batch", None)),
        check_vma=False,
    )
```

```python
import jax
import jax.numpy as jnp
from jax import lax
from jax.sharding import PartitionSpec as P
from jax.experimental import pallas as pl
from jax.experimental.pallas import tpu as pltpu


def _grad_payload_kernel(s_ref, g_ref, o_ref):
    peers, group, _ = o_ref.shape
    width = g_ref.shape[-1]
    for k in range(s_ref.shape[0]):
        product = lax.dot_general(
            g_ref[k], s_ref[k], (((0,), (0,)), ((), ())), preferred_element_type=jnp.float32
        ).T
        o_ref[:, :, k * width : (k + 1) * width] = product.reshape(peers, group, width).astype(o_ref.dtype)


def grad_payload(second_factor, upstream, peers):
    col_blocks, rows, order = second_factor.shape
    width = upstream.shape[-1]
    flops = 2 * col_blocks * rows * order * width
    return pl.pallas_call(
        _grad_payload_kernel,
        out_shape=jax.ShapeDtypeStruct((peers, order // peers, col_blocks * width), jnp.bfloat16),
        in_specs=[pl.BlockSpec(memory_space=pltpu.VMEM)] * 2,
        out_specs=pl.BlockSpec(memory_space=pltpu.VMEM),
        cost_estimate=pl.CostEstimate(
            flops=flops, transcendentals=0, bytes_accessed=2 * (second_factor.size + 2 * upstream.size)
        ),
    )(second_factor, upstream.reshape(col_blocks, rows, width))


def passed_along(value, axis, steps):
    count = lax.axis_size(axis)
    initial, last = (max(0, -steps), min(count, count - steps))
    return lax.ppermute(value, axis, [(source, source + steps) for source in range(initial, last)])


def body(signal, conv_weight, first_factor, second_factor, grad_output):
    seq_count, tok_rows, channels = signal.shape
    blocks = first_factor.shape[0]
    block_order = first_factor.shape[1]
    col_blocks = second_factor.shape[0]
    block_count = second_factor.shape[1]
    tap_count = conv_weight.shape[0]
    peers = lax.axis_size("seq")
    previous = passed_along(signal[:, tok_rows - (tap_count - 1) :, :], "seq", 1)
    padded_in = jnp.concatenate([previous, signal], axis=1).astype(jnp.float32)
    conv_out = sum(
        (
            conv_weight[r][None, None, :]
            * padded_in[:, tap_count - 1 - r : tap_count - 1 - r + tok_rows, :]
            for r in range(tap_count)
        )
    )
    gate_val = jax.nn.sigmoid(conv_out)
    hidden = (conv_out * gate_val).astype(jnp.bfloat16)
    hidden_blocks = hidden.reshape(seq_count, blocks, block_order, channels)
    first_split = first_factor.reshape(blocks, peers, col_blocks, block_order)
    mixed_chunks = jnp.einsum(
        "ipqj,sijd->psqid", first_split, hidden_blocks, preferred_element_type=jnp.float32
    ).astype(jnp.bfloat16)
    upstream = grad_output.reshape(seq_count, col_blocks, block_count, channels)
    grad_chunks = grad_payload(second_factor, upstream, peers)
    grad_rows = lax.all_to_all(grad_chunks, "seq", split_axis=0, concat_axis=0, tiled=True).reshape(
        peers, seq_count, blocks, col_blocks, channels
    )
    columns = lax.all_to_all(mixed_chunks, "seq", split_axis=0, concat_axis=3, tiled=True)[0]
    halves = lax.axis_size("batch")
    me = lax.axis_index("batch")
    other = halves - 1 - me
    rows_half = block_count // halves
    peers_half = peers // halves

    def second_part(half):
        up = lax.dynamic_slice_in_dim(upstream, half * rows_half, rows_half, 2)
        return jnp.einsum(
            "skmd,skid->kmi", up, columns, preferred_element_type=jnp.float32
        ).astype(jnp.bfloat16)

    def first_part(half):
        gr = lax.dynamic_slice_in_dim(grad_rows, half * peers_half, peers_half, 0)
        return jnp.einsum(
            "psiqd,sijd->ipqj", gr, hidden_blocks, preferred_element_type=jnp.float32
        ).reshape(blocks, peers_half * col_blocks, block_order).astype(jnp.bfloat16)

    swap = [(0, 1), (1, 0)]
    sent_second = lax.ppermute(second_part(other), "batch", swap)
    sent_first = lax.ppermute(first_part(other), "batch", swap)
    grad_hidden = jnp.einsum(
        "ipqj,psiqd->sijd", first_split, grad_rows, preferred_element_type=jnp.float32
    ).reshape(seq_count, tok_rows, channels)
    kept = lambda part: lax.reduce_precision(part.astype(jnp.float32), exponent_bits=8, mantissa_bits=7)
    own_second = lax.optimization_barrier(kept(second_part(me)))
    part_second = (own_second + sent_second.astype(jnp.float32)).astype(jnp.bfloat16)
    part_first = (kept(first_part(me)) + sent_first.astype(jnp.float32)).astype(jnp.bfloat16)
    grad_conv = (grad_hidden * gate_val * (1.0 + conv_out * (1.0 - gate_val))).astype(jnp.bfloat16)
    following = passed_along(grad_conv[:, : tap_count - 1, :], "seq", -1)
    extended = jnp.concatenate([grad_conv, following], axis=1).astype(jnp.float32)
    grad_signal = sum(
        (conv_weight[r][None, None, :] * extended[:, r : r + tok_rows, :] for r in range(tap_count))
    ).astype(jnp.bfloat16)
    return (grad_signal, part_first, part_second)


def solution(mesh):
    placed = (
        P("batch", "seq", None),
        P(),
        P("seq", None, None),
        P("seq", None, None),
        P("batch", "seq", None),
    )
    return jax.shard_map(
        body,
        mesh=mesh,
        in_specs=placed,
        out_specs=(P("batch", "seq", None), P("seq", "batch", None), P("seq", "batch", None)),
        check_vma=False,
    )
```

```python
import jax
import jax.numpy as jnp
from jax import lax
from jax.sharding import PartitionSpec as P
from jax.experimental import pallas as pl
from jax.experimental.pallas import tpu as pltpu


def _grad_payload_kernel(s_hbm, g_hbm, o_ref, s_vmem, g_vmem, sems):
    peers, group, _ = o_ref.shape
    col_blocks = s_hbm.shape[0]
    width = g_hbm.shape[-1]
    loads = []
    for k in range(col_blocks):
        pair = (
            pltpu.make_async_copy(s_hbm.at[k], s_vmem.at[k], sems.at[0, k]),
            pltpu.make_async_copy(g_hbm.at[k], g_vmem.at[k], sems.at[1, k]),
        )
        for copy in pair:
            copy.start()
        loads.append(pair)
    for k in range(col_blocks):
        for copy in loads[k]:
            copy.wait()
        product = lax.dot_general(
            s_vmem[k], g_vmem[k], (((0,), (0,)), ((), ())), preferred_element_type=jnp.float32
        )
        o_ref[:, :, k * width : (k + 1) * width] = product.reshape(peers, group, width).astype(o_ref.dtype)


def grad_payload(second_factor, upstream, peers):
    col_blocks, rows, order = second_factor.shape
    width = upstream.shape[-1]
    flops = 2 * col_blocks * rows * order * width
    return pl.pallas_call(
        _grad_payload_kernel,
        out_shape=jax.ShapeDtypeStruct((peers, order // peers, col_blocks * width), jnp.bfloat16),
        in_specs=[pl.BlockSpec(memory_space=pl.ANY)] * 2,
        out_specs=pl.BlockSpec(memory_space=pltpu.VMEM),
        scratch_shapes=[
            pltpu.VMEM((col_blocks, rows, order), jnp.bfloat16),
            pltpu.VMEM((col_blocks, rows, width), jnp.bfloat16),
            pltpu.SemaphoreType.DMA((2, col_blocks)),
        ],
        cost_estimate=pl.CostEstimate(
            flops=flops, transcendentals=0, bytes_accessed=2 * (second_factor.size + 2 * upstream.size)
        ),
    )(second_factor, upstream.reshape(col_blocks, rows, width))


def passed_along(value, axis, steps):
    count = lax.axis_size(axis)
    initial, last = (max(0, -steps), min(count, count - steps))
    return lax.ppermute(value, axis, [(source, source + steps) for source in range(initial, last)])


def body(signal, conv_weight, first_factor, second_factor, grad_output):
    seq_count, tok_rows, channels = signal.shape
    blocks = first_factor.shape[0]
    block_order = first_factor.shape[1]
    col_blocks = second_factor.shape[0]
    block_count = second_factor.shape[1]
    tap_count = conv_weight.shape[0]
    peers = lax.axis_size("seq")
    previous = passed_along(signal[:, tok_rows - (tap_count - 1) :, :], "seq", 1)
    padded_in = jnp.concatenate([previous, signal], axis=1).astype(jnp.float32)
    conv_out = sum(
        (
            conv_weight[r][None, None, :]
            * padded_in[:, tap_count - 1 - r : tap_count - 1 - r + tok_rows, :]
            for r in range(tap_count)
        )
    )
    gate_val = jax.nn.sigmoid(conv_out)
    hidden = (conv_out * gate_val).astype(jnp.bfloat16)
    hidden_blocks = hidden.reshape(seq_count, blocks, block_order, channels)
    first_split = first_factor.reshape(blocks, peers, col_blocks, block_order)
    mixed_chunks = jnp.einsum(
        "ipqj,sijd->psqid", first_split, hidden_blocks, preferred_element_type=jnp.float32
    ).astype(jnp.bfloat16)
    upstream = grad_output.reshape(seq_count, col_blocks, block_count, channels)
    grad_chunks = grad_payload(second_factor, upstream, peers)
    grad_rows = lax.all_to_all(grad_chunks, "seq", split_axis=0, concat_axis=0, tiled=True).reshape(
        peers, seq_count, blocks, col_blocks, channels
    )
    columns = lax.all_to_all(mixed_chunks, "seq", split_axis=0, concat_axis=3, tiled=True)[0]
    halves = lax.axis_size("batch")
    me = lax.axis_index("batch")
    other = halves - 1 - me
    rows_half = block_count // halves
    peers_half = peers // halves

    def second_part(half):
        up = lax.dynamic_slice_in_dim(upstream, half * rows_half, rows_half, 2)
        return jnp.einsum(
            "skmd,skid->kmi", up, columns, preferred_element_type=jnp.float32
        ).astype(jnp.bfloat16)

    def first_part(half):
        gr = lax.dynamic_slice_in_dim(grad_rows, half * peers_half, peers_half, 0)
        return jnp.einsum(
            "psiqd,sijd->ipqj", gr, hidden_blocks, preferred_element_type=jnp.float32
        ).reshape(blocks, peers_half * col_blocks, block_order).astype(jnp.bfloat16)

    swap = [(0, 1), (1, 0)]
    sent_second = lax.ppermute(second_part(other), "batch", swap)
    sent_first = lax.ppermute(first_part(other), "batch", swap)
    grad_hidden = jnp.einsum(
        "ipqj,psiqd->sijd", first_split, grad_rows, preferred_element_type=jnp.float32
    ).reshape(seq_count, tok_rows, channels)
    kept = lambda part: lax.reduce_precision(part.astype(jnp.float32), exponent_bits=8, mantissa_bits=7)
    own_second = lax.optimization_barrier(kept(second_part(me)))
    part_second = (own_second + sent_second.astype(jnp.float32)).astype(jnp.bfloat16)
    part_first = (kept(first_part(me)) + sent_first.astype(jnp.float32)).astype(jnp.bfloat16)
    grad_conv = (grad_hidden * gate_val * (1.0 + conv_out * (1.0 - gate_val))).astype(jnp.bfloat16)
    following = passed_along(grad_conv[:, : tap_count - 1, :], "seq", -1)
    extended = jnp.concatenate([grad_conv, following], axis=1).astype(jnp.float32)
    grad_signal = sum(
        (conv_weight[r][None, None, :] * extended[:, r : r + tok_rows, :] for r in range(tap_count))
    ).astype(jnp.bfloat16)
    return (grad_signal, part_first, part_second)


def solution(mesh):
    placed = (
        P("batch", "seq", None),
        P(),
        P("seq", None, None),
        P("seq", None, None),
        P("batch", "seq", None),
    )
    return jax.shard_map(
        body,
        mesh=mesh,
        in_specs=placed,
        out_specs=(P("batch", "seq", None), P("seq", "batch", None), P("seq", "batch", None)),
        check_vma=False,
    )
```

```python
import jax
import jax.numpy as jnp
from jax import lax
from jax.sharding import PartitionSpec as P
from jax.experimental import pallas as pl
from jax.experimental.pallas import tpu as pltpu


def _grad_payload_kernel(s_hbm, g_hbm, o_hbm, s_vmem, g_vmem, o_vmem, sems):
    col_blocks, peers, group, _ = o_vmem.shape
    width = g_hbm.shape[-1]
    loads = []
    for k in range(col_blocks):
        pair = (
            pltpu.make_async_copy(s_hbm.at[k], s_vmem.at[k], sems.at[0, k]),
            pltpu.make_async_copy(g_hbm.at[k], g_vmem.at[k], sems.at[1, k]),
        )
        for copy in pair:
            copy.start()
        loads.append(pair)
    stores = []
    for k in range(col_blocks):
        for copy in loads[k]:
            copy.wait()
        product = lax.dot_general(
            s_vmem[k], g_vmem[k], (((0,), (0,)), ((), ())), preferred_element_type=jnp.float32
        )
        o_vmem[k] = product.reshape(peers, group, width).astype(o_vmem.dtype)
        store = pltpu.make_async_copy(
            o_vmem.at[k], o_hbm.at[:, :, pl.ds(k * width, width)], sems.at[2, k]
        )
        store.start()
        stores.append(store)
    for store in stores:
        store.wait()


def grad_payload(second_factor, upstream, peers):
    col_blocks, rows, order = second_factor.shape
    width = upstream.shape[-1]
    flops = 2 * col_blocks * rows * order * width
    return pl.pallas_call(
        _grad_payload_kernel,
        out_shape=jax.ShapeDtypeStruct((peers, order // peers, col_blocks * width), jnp.bfloat16),
        in_specs=[pl.BlockSpec(memory_space=pl.ANY)] * 2,
        out_specs=pl.BlockSpec(memory_space=pl.ANY),
        scratch_shapes=[
            pltpu.VMEM((col_blocks, rows, order), jnp.bfloat16),
            pltpu.VMEM((col_blocks, rows, width), jnp.bfloat16),
            pltpu.VMEM((col_blocks, peers, order // peers, width), jnp.bfloat16),
            pltpu.SemaphoreType.DMA((3, col_blocks)),
        ],
        cost_estimate=pl.CostEstimate(
            flops=flops, transcendentals=0, bytes_accessed=2 * (second_factor.size + 2 * upstream.size)
        ),
    )(second_factor, upstream.reshape(col_blocks, rows, width))


def passed_along(value, axis, steps):
    count = lax.axis_size(axis)
    initial, last = (max(0, -steps), min(count, count - steps))
    return lax.ppermute(value, axis, [(source, source + steps) for source in range(initial, last)])


def body(signal, conv_weight, first_factor, second_factor, grad_output):
    seq_count, tok_rows, channels = signal.shape
    blocks = first_factor.shape[0]
    block_order = first_factor.shape[1]
    col_blocks = second_factor.shape[0]
    block_count = second_factor.shape[1]
    tap_count = conv_weight.shape[0]
    peers = lax.axis_size("seq")
    previous = passed_along(signal[:, tok_rows - (tap_count - 1) :, :], "seq", 1)
    padded_in = jnp.concatenate([previous, signal], axis=1).astype(jnp.float32)
    conv_out = sum(
        (
            conv_weight[r][None, None, :]
            * padded_in[:, tap_count - 1 - r : tap_count - 1 - r + tok_rows, :]
            for r in range(tap_count)
        )
    )
    gate_val = jax.nn.sigmoid(conv_out)
    hidden = (conv_out * gate_val).astype(jnp.bfloat16)
    hidden_blocks = hidden.reshape(seq_count, blocks, block_order, channels)
    first_split = first_factor.reshape(blocks, peers, col_blocks, block_order)
    mixed_chunks = jnp.einsum(
        "ipqj,sijd->psqid", first_split, hidden_blocks, preferred_element_type=jnp.float32
    ).astype(jnp.bfloat16)
    upstream = grad_output.reshape(seq_count, col_blocks, block_count, channels)
    grad_chunks = grad_payload(second_factor, upstream, peers)
    grad_rows = lax.all_to_all(grad_chunks, "seq", split_axis=0, concat_axis=0, tiled=True).reshape(
        peers, seq_count, blocks, col_blocks, channels
    )
    columns = lax.all_to_all(mixed_chunks, "seq", split_axis=0, concat_axis=3, tiled=True)[0]
    halves = lax.axis_size("batch")
    me = lax.axis_index("batch")
    other = halves - 1 - me
    rows_half = block_count // halves
    peers_half = peers // halves

    def second_part(half):
        up = lax.dynamic_slice_in_dim(upstream, half * rows_half, rows_half, 2)
        return jnp.einsum(
            "skmd,skid->kmi", up, columns, preferred_element_type=jnp.float32
        ).astype(jnp.bfloat16)

    def first_part(half):
        gr = lax.dynamic_slice_in_dim(grad_rows, half * peers_half, peers_half, 0)
        return jnp.einsum(
            "psiqd,sijd->ipqj", gr, hidden_blocks, preferred_element_type=jnp.float32
        ).reshape(blocks, peers_half * col_blocks, block_order).astype(jnp.bfloat16)

    swap = [(0, 1), (1, 0)]
    sent_second = lax.ppermute(second_part(other), "batch", swap)
    sent_first = lax.ppermute(first_part(other), "batch", swap)
    grad_hidden = jnp.einsum(
        "ipqj,psiqd->sijd", first_split, grad_rows, preferred_element_type=jnp.float32
    ).reshape(seq_count, tok_rows, channels)
    kept = lambda part: lax.reduce_precision(part.astype(jnp.float32), exponent_bits=8, mantissa_bits=7)
    own_second = lax.optimization_barrier(kept(second_part(me)))
    part_second = (own_second + sent_second.astype(jnp.float32)).astype(jnp.bfloat16)
    part_first = (kept(first_part(me)) + sent_first.astype(jnp.float32)).astype(jnp.bfloat16)
    grad_conv = (grad_hidden * gate_val * (1.0 + conv_out * (1.0 - gate_val))).astype(jnp.bfloat16)
    following = passed_along(grad_conv[:, : tap_count - 1, :], "seq", -1)
    extended = jnp.concatenate([grad_conv, following], axis=1).astype(jnp.float32)
    grad_signal = sum(
        (conv_weight[r][None, None, :] * extended[:, r : r + tok_rows, :] for r in range(tap_count))
    ).astype(jnp.bfloat16)
    return (grad_signal, part_first, part_second)


def solution(mesh):
    placed = (
        P("batch", "seq", None),
        P(),
        P("seq", None, None),
        P("seq", None, None),
        P("batch", "seq", None),
    )
    return jax.shard_map(
        body,
        mesh=mesh,
        in_specs=placed,
        out_specs=(P("batch", "seq", None), P("seq", "batch", None), P("seq", "batch", None)),
        check_vma=False,
    )
```

```python
import jax
import jax.numpy as jnp
from jax import lax
from jax.sharding import PartitionSpec as P
from jax.experimental import pallas as pl
from jax.experimental.pallas import tpu as pltpu


def _grad_payload_kernel(s_hbm, g_hbm, o_ref, s_vmem, g_vmem, sems):
    peers, group, _ = o_ref.shape
    col_blocks = s_hbm.shape[0]
    width = g_hbm.shape[-1]
    loads = []
    for k in range(col_blocks):
        pair = (
            pltpu.make_async_copy(s_hbm.at[k], s_vmem.at[k], sems.at[0, k]),
            pltpu.make_async_copy(g_hbm.at[k], g_vmem.at[k], sems.at[1, k]),
        )
        for copy in pair:
            copy.start()
        loads.append(pair)
    for k in range(col_blocks):
        for copy in loads[k]:
            copy.wait()
        product = lax.dot_general(
            s_vmem[k], g_vmem[k], (((0,), (0,)), ((), ())), preferred_element_type=jnp.float32
        )
        o_ref[:, :, k * width : (k + 1) * width] = product.reshape(peers, group, width).astype(o_ref.dtype)


def grad_payload(second_factor, upstream, peers):
    col_blocks, rows, order = second_factor.shape
    width = upstream.shape[-1]
    flops = 2 * col_blocks * rows * order * width
    return pl.pallas_call(
        _grad_payload_kernel,
        out_shape=jax.ShapeDtypeStruct((peers, order // peers, col_blocks * width), jnp.bfloat16),
        in_specs=[pl.BlockSpec(memory_space=pl.ANY)] * 2,
        out_specs=pl.BlockSpec(memory_space=pltpu.VMEM),
        scratch_shapes=[
            pltpu.VMEM((col_blocks, rows, order), jnp.bfloat16),
            pltpu.VMEM((col_blocks, rows, width), jnp.bfloat16),
            pltpu.SemaphoreType.DMA((2, col_blocks)),
        ],
        cost_estimate=pl.CostEstimate(
            flops=flops, transcendentals=0, bytes_accessed=2 * (second_factor.size + 2 * upstream.size)
        ),
    )(second_factor, upstream.reshape(col_blocks, rows, width))


def passed_along(value, axis, steps):
    count = lax.axis_size(axis)
    initial, last = (max(0, -steps), min(count, count - steps))
    return lax.ppermute(value, axis, [(source, source + steps) for source in range(initial, last)])


def body(signal, conv_weight, first_factor, second_factor, grad_output):
    seq_count, tok_rows, channels = signal.shape
    blocks = first_factor.shape[0]
    block_order = first_factor.shape[1]
    col_blocks = second_factor.shape[0]
    block_count = second_factor.shape[1]
    tap_count = conv_weight.shape[0]
    peers = lax.axis_size("seq")
    previous = passed_along(signal[:, tok_rows - (tap_count - 1) :, :], "seq", 1)
    padded_in = jnp.concatenate([previous, signal], axis=1).astype(jnp.float32)
    conv_out = sum(
        (
            conv_weight[r][None, None, :]
            * padded_in[:, tap_count - 1 - r : tap_count - 1 - r + tok_rows, :]
            for r in range(tap_count)
        )
    )
    gate_val = jax.nn.sigmoid(conv_out)
    hidden = (conv_out * gate_val).astype(jnp.bfloat16)
    hidden_blocks = hidden.reshape(seq_count, blocks, block_order, channels)
    first_split = first_factor.reshape(blocks, peers, col_blocks, block_order)
    mixed_chunks = jnp.einsum(
        "ipqj,sijd->psqid", first_split, hidden_blocks, preferred_element_type=jnp.float32
    ).astype(jnp.bfloat16)
    upstream = grad_output.reshape(seq_count, col_blocks, block_count, channels)
    grad_chunks = grad_payload(second_factor, upstream, peers)
    grad_rows = lax.all_to_all(grad_chunks, "seq", split_axis=0, concat_axis=0, tiled=True).reshape(
        peers, seq_count, blocks, col_blocks, channels
    )
    columns = lax.all_to_all(mixed_chunks, "seq", split_axis=0, concat_axis=3, tiled=True)[0]
    halves = lax.axis_size("batch")
    me = lax.axis_index("batch")
    other = halves - 1 - me
    rows_half = block_count // halves
    peers_half = peers // halves

    def second_part(half):
        up = lax.dynamic_slice_in_dim(upstream, half * rows_half, rows_half, 2)
        return jnp.einsum(
            "skmd,skid->kmi", up, columns, preferred_element_type=jnp.float32
        ).astype(jnp.bfloat16)

    def first_part(half):
        gr = lax.dynamic_slice_in_dim(grad_rows, half * peers_half, peers_half, 0)
        return jnp.einsum(
            "psiqd,sijd->ipqj", gr, hidden_blocks, preferred_element_type=jnp.float32
        ).reshape(blocks, peers_half * col_blocks, block_order).astype(jnp.bfloat16)

    swap = [(0, 1), (1, 0)]
    sent_second = lax.ppermute(second_part(other), "batch", swap)
    sent_first = lax.ppermute(first_part(other), "batch", swap)
    grad_hidden = jnp.einsum(
        "ipqj,psiqd->sijd", first_split, grad_rows, preferred_element_type=jnp.float32
    ).reshape(seq_count, tok_rows, channels)
    kept = lambda part: lax.reduce_precision(part.astype(jnp.float32), exponent_bits=8, mantissa_bits=7)
    own_second = lax.optimization_barrier(second_part(me))
    part_second = (own_second.astype(jnp.float32) + sent_second.astype(jnp.float32)).astype(jnp.bfloat16)
    part_first = (kept(first_part(me)) + sent_first.astype(jnp.float32)).astype(jnp.bfloat16)
    grad_conv = (grad_hidden * gate_val * (1.0 + conv_out * (1.0 - gate_val))).astype(jnp.bfloat16)
    following = passed_along(grad_conv[:, : tap_count - 1, :], "seq", -1)
    extended = jnp.concatenate([grad_conv, following], axis=1).astype(jnp.float32)
    grad_signal = sum(
        (conv_weight[r][None, None, :] * extended[:, r : r + tok_rows, :] for r in range(tap_count))
    ).astype(jnp.bfloat16)
    return (grad_signal, part_first, part_second)


def solution(mesh):
    placed = (
        P("batch", "seq", None),
        P(),
        P("seq", None, None),
        P("seq", None, None),
        P("batch", "seq", None),
    )
    return jax.shard_map(
        body,
        mesh=mesh,
        in_specs=placed,
        out_specs=(P("batch", "seq", None), P("seq", "batch", None), P("seq", "batch", None)),
        check_vma=False,
    )
```

```python
import jax
import jax.numpy as jnp
from jax import lax
from jax.sharding import PartitionSpec as P
from jax.experimental import pallas as pl
from jax.experimental.pallas import tpu as pltpu


def _grad_payload_kernel(s_hbm, g_hbm, o_hbm, s_vmem, g_vmem, o_vmem, sems):
    col_blocks, peers, group, _ = o_vmem.shape
    width = g_hbm.shape[-1]
    loads = []
    for k in range(col_blocks):
        pair = (
            pltpu.make_async_copy(s_hbm.at[k], s_vmem.at[k], sems.at[0, k]),
            pltpu.make_async_copy(g_hbm.at[k], g_vmem.at[k], sems.at[1, k]),
        )
        for copy in pair:
            copy.start()
        loads.append(pair)
    stores = []
    for k in range(col_blocks):
        for copy in loads[k]:
            copy.wait()
        product = lax.dot_general(
            s_vmem[k], g_vmem[k], (((0,), (0,)), ((), ())), preferred_element_type=jnp.float32
        )
        o_vmem[k] = product.reshape(peers, group, width).astype(o_vmem.dtype)
        store = pltpu.make_async_copy(
            o_vmem.at[k], o_hbm.at[:, :, pl.ds(k * width, width)], sems.at[2, k]
        )
        store.start()
        stores.append(store)
    for store in stores:
        store.wait()


def grad_payload(second_factor, upstream, peers):
    col_blocks, rows, order = second_factor.shape
    width = upstream.shape[-1]
    flops = 2 * col_blocks * rows * order * width
    return pl.pallas_call(
        _grad_payload_kernel,
        out_shape=jax.ShapeDtypeStruct((peers, order // peers, col_blocks * width), jnp.bfloat16),
        in_specs=[pl.BlockSpec(memory_space=pl.ANY)] * 2,
        out_specs=pl.BlockSpec(memory_space=pl.ANY),
        scratch_shapes=[
            pltpu.VMEM((col_blocks, rows, order), jnp.bfloat16),
            pltpu.VMEM((col_blocks, rows, width), jnp.bfloat16),
            pltpu.VMEM((col_blocks, peers, order // peers, width), jnp.bfloat16),
            pltpu.SemaphoreType.DMA((3, col_blocks)),
        ],
        cost_estimate=pl.CostEstimate(
            flops=flops, transcendentals=0, bytes_accessed=2 * (second_factor.size + 2 * upstream.size)
        ),
    )(second_factor, upstream.reshape(col_blocks, rows, width))


def passed_along(value, axis, steps):
    count = lax.axis_size(axis)
    initial, last = (max(0, -steps), min(count, count - steps))
    return lax.ppermute(value, axis, [(source, source + steps) for source in range(initial, last)])


def body(signal, conv_weight, first_factor, second_factor, grad_output):
    seq_count, tok_rows, channels = signal.shape
    blocks = first_factor.shape[0]
    block_order = first_factor.shape[1]
    col_blocks = second_factor.shape[0]
    block_count = second_factor.shape[1]
    tap_count = conv_weight.shape[0]
    peers = lax.axis_size("seq")
    previous = passed_along(signal[:, tok_rows - (tap_count - 1) :, :], "seq", 1)
    padded_in = jnp.concatenate([previous, signal], axis=1).astype(jnp.float32)
    conv_out = sum(
        (
            conv_weight[r][None, None, :]
            * padded_in[:, tap_count - 1 - r : tap_count - 1 - r + tok_rows, :]
            for r in range(tap_count)
        )
    )
    gate_val = jax.nn.sigmoid(conv_out)
    hidden = (conv_out * gate_val).astype(jnp.bfloat16)
    hidden_blocks = hidden.reshape(seq_count, blocks, block_order, channels)
    first_split = first_factor.reshape(blocks, peers, col_blocks, block_order)
    mixed_chunks = jnp.einsum(
        "ipqj,sijd->psqid", first_split, hidden_blocks, preferred_element_type=jnp.float32
    ).astype(jnp.bfloat16)
    upstream = grad_output.reshape(seq_count, col_blocks, block_count, channels)
    grad_chunks = grad_payload(second_factor, upstream, peers)
    grad_rows = lax.all_to_all(grad_chunks, "seq", split_axis=0, concat_axis=0, tiled=True).reshape(
        peers, seq_count, blocks, col_blocks, channels
    )
    columns = lax.all_to_all(mixed_chunks, "seq", split_axis=0, concat_axis=3, tiled=True)[0]
    halves = lax.axis_size("batch")
    me = lax.axis_index("batch")
    other = halves - 1 - me
    rows_half = block_count // halves
    peers_half = peers // halves

    def second_part(half):
        up = lax.dynamic_slice_in_dim(upstream, half * rows_half, rows_half, 2)
        return jnp.einsum(
            "skmd,skid->kmi", up, columns, preferred_element_type=jnp.float32
        ).astype(jnp.bfloat16)

    def first_part(half):
        gr = lax.dynamic_slice_in_dim(grad_rows, half * peers_half, peers_half, 0)
        return jnp.einsum(
            "psiqd,sijd->ipqj", gr, hidden_blocks, preferred_element_type=jnp.float32
        ).reshape(blocks, peers_half * col_blocks, block_order).astype(jnp.bfloat16)

    swap = [(0, 1), (1, 0)]
    sent_second = lax.ppermute(second_part(other), "batch", swap)
    sent_first = lax.ppermute(first_part(other), "batch", swap)
    grad_hidden = jnp.einsum(
        "ipqj,psiqd->sijd", first_split, grad_rows, preferred_element_type=jnp.float32
    ).reshape(seq_count, tok_rows, channels)
    kept = lambda part: lax.reduce_precision(part.astype(jnp.float32), exponent_bits=8, mantissa_bits=7)
    own_second = lax.optimization_barrier(second_part(me))
    part_second = (own_second.astype(jnp.float32) + sent_second.astype(jnp.float32)).astype(jnp.bfloat16)
    part_first = (kept(first_part(me)) + sent_first.astype(jnp.float32)).astype(jnp.bfloat16)
    grad_conv = (grad_hidden * gate_val * (1.0 + conv_out * (1.0 - gate_val))).astype(jnp.bfloat16)
    following = passed_along(grad_conv[:, : tap_count - 1, :], "seq", -1)
    extended = jnp.concatenate([grad_conv, following], axis=1).astype(jnp.float32)
    grad_signal = sum(
        (conv_weight[r][None, None, :] * extended[:, r : r + tok_rows, :] for r in range(tap_count))
    ).astype(jnp.bfloat16)
    return (grad_signal, part_first, part_second)


def solution(mesh):
    placed = (
        P("batch", "seq", None),
        P(),
        P("seq", None, None),
        P("seq", None, None),
        P("batch", "seq", None),
    )
    return jax.shard_map(
        body,
        mesh=mesh,
        in_specs=placed,
        out_specs=(P("batch", "seq", None), P("seq", "batch", None), P("seq", "batch", None)),
        check_vma=False,
    )
```
